128 devices in a mesh: src: 8 (over y, x_lo), vox: 16 (over x_hi, z, core).
Axes of the slice: x: 4 (x_hi: 2, x_lo: 2; x = x_hi * 2 + x_lo), y: 4, z: 4, core: 2. Of those that a mesh axis runs over, the one named last changes fastest.
Arguments:
- kappa: float32 [128, 64, 256], P('vox'), may hold values from 0.3 to 3
- mua: float32 [128, 64, 256], P('vox'), may hold values from 0.1 to 2
- prior_forward_fields: float32 [16, 128, 64, 256], P('src', 'vox'), may hold values from -10 to 10
- prior_adjoint_fields: float32 [16, 128, 64, 256], P('src', 'vox'), may hold values from -10 to 10
- source_position: int32 [16], replicated, may hold values from 0 to 2097151
- detector_voxel: int32 [2048], P('vox'), may hold values from 0 to 2097151, as said below
- measured_source: int32 [131072], P(('src', 'vox')), may hold values from 0 to 15, as said below
- measured_detector: int32 [131072], P(('src', 'vox')), may hold values from 0 to 2047, as said below
- measured_data: float32 [131072], P(('src', 'vox')), may hold values from -6 to 6
- measured_weight: float32 [131072], P(('src', 'vox')), may hold values from 0.25 to 4
Outputs:
- grad_mua: float32 [128, 64, 256], P('vox', 'src')
- grad_kappa: float32 [128, 64, 256], P('vox', 'src')
The draws below stay inside these ranges and needn't reach their ends.
Inputs may be any that keep to these rules, and one draw needn't show every extreme that they name: `measured_source`: in each aligned block of 1024 rows (the rows of one device), at most 512 rows name a source of one group, a group being the 2 sources s with the same s // 2. `measured_detector`: row r names a detector of detector block (r // 1024) % 16, that is one from that block times 128 up to the next block's first. `detector_voxel`: detector d lies in the voxel planes x from (d // 128) * 8 to that plus 8 - 1.
All inputs are finite; a program needn't handle non-finite values.
Results may differ from the reference program's by a relative error of at most 0.0003.
Values sent between devices are 32-bit elements; how exact they have to be, the bound alone decides.
A program may use at most 256 MiB of HBM per device.

```python
import math
import jax
import jax.numpy as jnp
from jax import lax

CX = 8
NY = 64
NZ = 256
SWEEPS = 6
SRC_DEV = 2
DET_DEV = 128
ROWS_DEV = 1024
NX = 128
NSRC = 16
DETECTOR_COUNT = 2048
MEASURE_ROWS = 131072


def draw_measured_source(key, part):
    block_count = MEASURE_ROWS // ROWS_DEV
    vox_count = DETECTOR_COUNT // DET_DEV
    group_count = NSRC // SRC_DEV
    slot_capacity = ROWS_DEV // 2
    key_busy, key_other, key_order, key_member = jax.random.split(key, 4)
    busiest = jax.random.randint(key_busy, (vox_count,), 0, group_count)
    column = jnp.arange(block_count) % vox_count
    block_busy = busiest[column]
    slots = jnp.arange(ROWS_DEV)
    others = jax.random.randint(key_other, (block_count, ROWS_DEV), 0, group_count - 1)
    others = others + (others >= block_busy[:, None]).astype(jnp.int32)
    chosen = jnp.where(slots[None, :] < slot_capacity, block_busy[:, None], others)
    scores = jax.random.randint(key_order, (block_count, ROWS_DEV), 0, 1 << 18) * ROWS_DEV + slots[None, :]
    order = jnp.argsort(scores, axis=1, stable=True)
    chosen = jnp.take_along_axis(chosen, order, axis=1)
    member = jax.random.randint(key_member, (block_count, ROWS_DEV), 0, SRC_DEV)
    return (chosen * SRC_DEV + member).reshape(-1).astype(jnp.int32)


def draw_measured_detector(key, part):
    vox_count = DETECTOR_COUNT // DET_DEV
    column = jnp.arange(MEASURE_ROWS) // ROWS_DEV % vox_count
    within = jax.random.randint(key, (MEASURE_ROWS,), 0, DET_DEV)
    return (column * DET_DEV + within).astype(jnp.int32)


def draw_detector_voxel(key, part):
    key_x, key_y, key_z = jax.random.split(key, 3)
    slab_position_index = jnp.arange(DETECTOR_COUNT) // DET_DEV
    plane_x = slab_position_index * CX + jax.random.randint(key_x, (DETECTOR_COUNT,), 0, CX)
    plane_y = jax.random.randint(key_y, (DETECTOR_COUNT,), 0, NY)
    plane_z = jax.random.randint(key_z, (DETECTOR_COUNT,), 0, NZ)
    return ((plane_x * NY + plane_y) * NZ + plane_z).astype(jnp.int32)


def set_ends(drawn, stream_key, low, top_value):
    longest = drawn.shape.index(max(drawn.shape))
    spots = []
    for shift in (0, 1):
        where = [jax.random.randint(jax.random.fold_in(stream_key, axis), (), 0, length) for axis, length in enumerate(drawn.shape)]
        where[longest] = (where[longest] + shift) % drawn.shape[longest]
        spots.append(tuple(where))
    return drawn.at[spots[0]].set(low).at[spots[1]].set(top_value)


def block_levels(key, extent, shards, low, high):
    factor_of, own = 1.0, jax.random.fold_in(key, 6)
    for position, parts in shards:
        steps = jnp.exp(jax.random.uniform(jax.random.fold_in(own, position), (parts,), jnp.float32, low / len(shards), high / len(shards)))
        factor_of = factor_of * jnp.repeat(steps, extent[position] // parts).reshape([-1 if axis == position else 1 for axis in range(len(extent))])
    return factor_of


def centred(rng, dims, width, limit, pieces=(), kind=jnp.bfloat16):
    result = width * jax.random.normal(rng, dims, jnp.float32)
    if pieces:
        result = result * block_levels(rng, dims, pieces, -0.22, 0.18)
    return jnp.clip(result, -limit, limit).astype(kind)


def setup_inputs(seed: int = 0) -> dict:
    keys = jax.random.split(jax.random.key(seed), 11)
    kappa = jnp.clip(jnp.exp(math.log(3.0) - 2.3025851 * jax.random.uniform(keys[0], (NX, NY, NZ), jnp.float32) ** block_levels(keys[0], (NX, NY, NZ), ((0, 16),), -0.2, 0.2)), 0.3, 3.0)
    mua = jnp.clip(jnp.exp(math.log(2.0) - 2.9957323 * jax.random.uniform(keys[1], (NX, NY, NZ), jnp.float32) ** block_levels(keys[1], (NX, NY, NZ), ((0, 16),), -0.2, 0.2)), 0.1, 2.0)
    prior_forward_fields = centred(keys[2], (NSRC, NX, NY, NZ), 2.0, 10.0, ((0, 8), (1, 16)), jnp.float32)
    prior_adjoint_fields = centred(keys[3], (NSRC, NX, NY, NZ), 2.0, 10.0, ((0, 8), (1, 16)), jnp.float32)
    source_position = set_ends(jax.random.randint(keys[4], (NSRC,), 0, NX * NY * NZ), jax.random.fold_in(keys[4], 1), 0, (NX * NY * NZ) - 1).astype(jnp.int32)
    detector_voxel = draw_detector_voxel(jax.random.fold_in(keys[10], 71), 0)
    measured_source = draw_measured_source(jax.random.fold_in(keys[10], 71), 0)
    measured_detector = draw_measured_detector(jax.random.fold_in(keys[10], 71), 0)
    measured_data = centred(keys[8], (MEASURE_ROWS,), 1.0, 6.0, ((0, 128),), jnp.float32)
    measured_weight = jnp.clip(jnp.exp(math.log(4.0) - 2.7725887 * jax.random.uniform(keys[9], (MEASURE_ROWS,), jnp.float32) ** block_levels(keys[9], (MEASURE_ROWS,), ((0, 128),), -0.2, 0.2)), 0.25, 4.0)
    return dict(kappa=kappa, mua=mua, prior_forward_fields=prior_forward_fields, prior_adjoint_fields=prior_adjoint_fields, source_position=source_position, detector_voxel=detector_voxel, measured_source=measured_source, measured_detector=measured_detector, measured_data=measured_data, measured_weight=measured_weight)


source_gain = 10.0


def conductances(kappa):
    padded = jnp.pad(kappa, 1)
    face_x = 0.5 * (padded[1:, 1:-1, 1:-1] + padded[:-1, 1:-1, 1:-1])
    face_y = 0.5 * (padded[1:-1, 1:, 1:-1] + padded[1:-1, :-1, 1:-1])
    face_z = 0.5 * (padded[1:-1, 1:-1, 1:] + padded[1:-1, 1:-1, :-1])
    return face_x, face_y, face_z


def jacobi_sweep(current, source, face_x, face_y, face_z, diagonal):
    padded = jnp.pad(current, 1)
    inflow = face_x[1:] * padded[2:, 1:-1, 1:-1] + face_x[:-1] * padded[:-2, 1:-1, 1:-1]
    inflow = inflow + face_y[:, 1:] * padded[1:-1, 2:, 1:-1] + face_y[:, :-1] * padded[1:-1, :-2, 1:-1]
    inflow = inflow + face_z[:, :, 1:] * padded[1:-1, 1:-1, 2:] + face_z[:, :, :-1] * padded[1:-1, 1:-1, :-2]
    return (source + inflow) / diagonal


def along(values, axis):
    upper = lax.slice_in_dim(values, 1, values.shape[axis], axis=axis)
    edge = jnp.zeros_like(lax.slice_in_dim(values, 0, 1, axis=axis))
    return jnp.concatenate([upper, edge], axis=axis) - values


def reference(kappa, mua, prior_forward_fields, prior_adjoint_fields, source_position, detector_voxel, measured_source, measured_detector, measured_data, measured_weight):
    face_x, face_y, face_z = conductances(kappa)
    diagonal = mua + face_x[1:] + face_x[:-1] + face_y[:, 1:] + face_y[:, :-1] + face_z[:, :, 1:] + face_z[:, :, :-1]
    cell_total = NX * NY * NZ

    def one_source(carry, inputs):
        grad_mua, grad_kappa = carry
        source_number, start_fwd, start_adj = inputs
        source = jnp.zeros((cell_total,), jnp.float32).at[source_position[source_number]].set(source_gain).reshape(NX, NY, NZ)
        forward = start_fwd
        for sweep in range(SWEEPS):
            forward = jacobi_sweep(forward, source, face_x, face_y, face_z, diagonal)
        predicted_value = forward.reshape(-1)[detector_voxel]
        residual_value = jnp.where(measured_source == source_number, measured_weight * (predicted_value[measured_detector] - measured_data), 0.0)
        detector_totals = jax.ops.segment_sum(residual_value, measured_detector, num_segments=DETECTOR_COUNT)
        back_source = jnp.zeros((cell_total,), jnp.float32).at[detector_voxel].add(detector_totals).reshape(NX, NY, NZ)
        adjoint = start_adj
        for sweep in range(SWEEPS):
            adjoint = jacobi_sweep(adjoint, back_source, face_x, face_y, face_z, diagonal)
        grad_mua = grad_mua - forward * adjoint
        product = along(forward, 0) * along(adjoint, 0) + along(forward, 1) * along(adjoint, 1) + along(forward, 2) * along(adjoint, 2)
        grad_kappa = grad_kappa - product
        return (grad_mua, grad_kappa), None

    zeros_grid = jnp.zeros((NX, NY, NZ), jnp.float32)
    source_ids = jnp.arange(NSRC, dtype=jnp.int32)
    (grad_mua, grad_kappa), unused = lax.scan(one_source, (zeros_grid, zeros_grid), (source_ids, prior_forward_fields, prior_adjoint_fields))
    return grad_mua, grad_kappa
```

```python
import functools

import jax
import jax.numpy as jnp
from jax import lax
from jax.experimental import pallas as pl
from jax.experimental.pallas import tpu as pltpu
from jax.sharding import PartitionSpec as P

SWEEPS = 6
LOW = SWEEPS
HIGH = SWEEPS + 1
source_gain = 10.0

MESH = pl.DeviceIdType.MESH
F32 = jnp.float32
BF16 = jnp.bfloat16
HI = lax.Precision.HIGHEST
NT = (((1,), (1,)), ((), ()))


def slots(ref, *lead):
    return jnp.stack([ref[(*lead, pl.ds(j, 8, stride=8), slice(None))] for j in range(8)])


def y_next(value, zero_edge):
    wrapped = pltpu.roll(value[:1], 7, 1)
    if zero_edge:
        rows = lax.broadcasted_iota(jnp.int32, wrapped.shape, 1)
        wrapped = jnp.where(rows == 7, 0.0, wrapped)
    return jnp.concatenate([value[1:], wrapped], axis=0)


def y_prev(value, zero_edge):
    wrapped = pltpu.roll(value[-1:], 1, 1)
    if zero_edge:
        rows = lax.broadcasted_iota(jnp.int32, wrapped.shape, 1)
        wrapped = jnp.where(rows == 0, 0.0, wrapped)
    return jnp.concatenate([wrapped, value[:-1]], axis=0)


def z_next(halves, zero_edge):
    lane = lax.broadcasted_iota(jnp.int32, halves[0].shape, halves[0].ndim - 1)
    turned = [pltpu.roll(half, 127, half.ndim - 1) for half in halves]
    last = jnp.where(lane == 127, 0.0, turned[1]) if zero_edge else turned[1]
    return [jnp.where(lane == 127, turned[1], turned[0]), last]


def z_prev(halves, zero_edge):
    lane = lax.broadcasted_iota(jnp.int32, halves[0].shape, halves[0].ndim - 1)
    turned = [pltpu.roll(half, 1, half.ndim - 1) for half in halves]
    first = jnp.where(lane == 0, 0.0, turned[0]) if zero_edge else turned[0]
    return [first, jnp.where(lane == 0, turned[0], turned[1])]


def three_parts(value):
    high = value.astype(BF16)
    rest = value - high.astype(F32)
    middle = rest.astype(BF16)
    low = (rest - middle.astype(F32)).astype(BF16)
    return high.astype(F32), middle.astype(F32), low.astype(F32)


def kernel(
    groups,
    slabs,
    kappa,
    mua,
    prior_fwd,
    prior_adj,
    position,
    det_scalar,
    det_row,
    row_source,
    row_detector,
    row_data,
    row_weight,
    out_mua,
    out_kappa,
    kap,
    mu,
    fwd_in,
    adj_in,
    field,
    other,
    adjf,
    coef,
    drive,
    agg,
    agg_in,
    val,
    val_in,
    det_in,
    zhot,
    picked,
    grad,
    grad_in,
    local_sem,
    halo_send,
    halo_recv,
    det_send,
    det_recv,
    agg_send,
    agg_recv,
    val_send,
    val_recv,
    grad_send,
    grad_recv,
):
    src = lax.axis_index("src")
    vox = lax.axis_index("vox")
    core = lax.rem(vox, 2)
    depth = kappa.shape[0]
    total = LOW + depth + HIGH
    detectors = det_row.shape[1]
    has_low = vox > 0
    has_high = vox < slabs - 1
    below = {"vox": jnp.maximum(vox - 1, 0)}
    above = {"vox": jnp.minimum(vox + 1, slabs - 1)}
    peers = [lax.rem(src + step, groups) for step in range(1, groups)]

    barrier = pltpu.get_barrier_semaphore()

    @pl.when(has_high)
    def _():
        pl.semaphore_signal(barrier, inc=1, device_id=above, device_id_type=MESH)

    @pl.when(has_low)
    def _():
        pl.semaphore_signal(barrier, inc=1, device_id=below, device_id_type=MESH)

    for peer in peers:
        pl.semaphore_signal(barrier, inc=1, device_id={"src": peer}, device_id_type=MESH)

    own = []
    for h in range(2):
        lanes = pl.ds(128 * h, 128)
        own.append(
            [
                pltpu.make_async_copy(
                    kappa.at[:, :, lanes], kap.at[pl.ds(LOW, depth), h], local_sem.at[0, h]
                ),
                pltpu.make_async_copy(
                    mua.at[:, :, lanes], mu.at[pl.ds(LOW, depth), h], local_sem.at[1, h]
                ),
                pltpu.make_async_copy(
                    prior_fwd.at[:, :, :, lanes],
                    fwd_in.at[:, pl.ds(LOW, depth), h],
                    local_sem.at[2, h],
                ),
                pltpu.make_async_copy(
                    prior_adj.at[:, :, :, lanes],
                    adj_in.at[:, pl.ds(LOW, depth), h],
                    local_sem.at[3, h],
                ),
            ]
        )
    for which in range(4):
        for h in range(2):
            own[h][which].start()

    pl.semaphore_wait(
        barrier, groups - 1 + jnp.where(has_low, 1, 0) + jnp.where(has_high, 1, 0)
    )

    def halo(array, direction, h):
        lanes = pl.ds(128 * h, 128)
        if direction == 0:
            count = LOW - 1 if array == 1 else LOW
            start, target = depth - count, LOW - count
        else:
            count = HIGH - 1 if array == 1 else HIGH
            start, target = 0, LOW + depth
        if array < 2:
            source = (kappa, mua)[array].at[pl.ds(start, count), :, lanes]
            place = (kap, mu)[array].at[pl.ds(target, count), h]
        else:
            source = (prior_fwd, prior_adj)[array - 2].at[:, pl.ds(start, count), :, lanes]
            place = (fwd_in, adj_in)[array - 2].at[:, pl.ds(target, count), h]
        return pltpu.make_async_remote_copy(
            src_ref=source,
            dst_ref=place,
            send_sem=halo_send.at[array, direction, h],
            recv_sem=halo_recv.at[array, direction, h],
            device_id=above if direction == 0 else below,
            device_id_type=MESH,
        )

    halos = [[[halo(a, d, h) for h in range(2)] for d in range(2)] for a in range(4)]
    det_copy = [
        pltpu.make_async_remote_copy(
            src_ref=det_row,
            dst_ref=det_in.at[d],
            send_sem=det_send.at[d],
            recv_sem=det_recv.at[d],
            device_id=(above, below)[d],
            device_id_type=MESH,
        )
        for d in range(2)
    ]

    sends_to = (has_high, has_low)
    gets_from = (has_low, has_high)
    for d in range(2):

        @pl.when(sends_to[d])
        def _():
            det_copy[d].start()
            for a in range(4):
                for h in range(2):
                    halos[a][d][h].start()

    for d in range(2):

        @pl.when(jnp.logical_not(gets_from[d]))
        def _():
            if d == 0:
                planes = slice(0, LOW)
            else:
                planes = slice(LOW + depth, total)
            kap[planes] = jnp.zeros_like(kap[planes])
            fwd_in[:, planes] = jnp.zeros_like(fwd_in[:, planes])
            adj_in[:, planes] = jnp.zeros_like(adj_in[:, planes])
            det_in[d] = jnp.zeros_like(det_in[d])
            val_in[d] = jnp.zeros_like(val_in[d])

    rows = lax.broadcasted_iota(jnp.int32, (8 * groups, 128), 0)
    kind = rows % 8
    source_of = rows // 8 * 2 + kind % 2
    det_base = vox * detectors
    det_ids = lax.broadcasted_iota(jnp.int32, (detectors, 128), 0) + det_base
    summed = jnp.zeros((8 * groups, detectors), F32)
    for i in range(row_source.shape[0]):
        weight = row_weight[i : i + 1, :]
        weighted = weight * row_data[i : i + 1, :]
        chosen = jnp.where(kind < 2, weight, jnp.where(kind < 4, weighted, 0.0))
        chosen = jnp.where(row_source[i : i + 1, :] == source_of, chosen, 0.0)
        hot = jnp.where(row_detector[i : i + 1, :] == det_ids, 1.0, 0.0)
        summed = summed + lax.dot_general(
            chosen, hot, NT, precision=HI, preferred_element_type=F32
        )
    agg[...] = summed
    agg_copy = []
    for step, peer in enumerate(peers):
        copy = pltpu.make_async_remote_copy(
            src_ref=agg.at[pl.ds(pl.multiple_of(8 * peer, 8), 8)],
            dst_ref=agg_in.at[src],
            send_sem=agg_send.at[step],
            recv_sem=agg_recv.at[step],
            device_id={"src": peer},
            device_id_type=MESH,
        )
        copy.start()
        agg_copy.append(copy)
    agg_in[src] = agg[pl.ds(pl.multiple_of(8 * src, 8), 8), :]

    def coefficients(low, count):
        def body(i, carry):
            p = low + i
            x = vox * depth + p - LOW
            inside = jnp.logical_and(x >= 0, x < slabs * depth)
            centre = [slots(kap, p, h) for h in range(2)]
            zn, zp = z_next(centre, True), z_prev(centre, True)
            row = lax.broadcasted_iota(jnp.int32, (8, 8, 128), 1) * 8 + lax.broadcasted_iota(
                jnp.int32, (8, 8, 128), 0
            )
            lane = lax.broadcasted_iota(jnp.int32, (8, 8, 128), 2)
            for h in range(2):
                mid = centre[h]
                faces = [
                    0.5 * (slots(kap, p + 1, h) + mid),
                    0.5 * (mid + slots(kap, p - 1, h)),
                    0.5 * (y_next(mid, True) + mid),
                    0.5 * (mid + y_prev(mid, True)),
                    0.5 * (zn[h] + mid),
                    0.5 * (mid + zp[h]),
                ]
                diagonal = slots(mu, p, h)
                for face in faces:
                    diagonal = diagonal + face
                inverse = jnp.where(inside, 1.0 / jnp.where(inside, diagonal, 1.0), 0.0)
                faces[2] = jnp.where(row == 63, 0.0, faces[2])
                faces[3] = jnp.where(row == 0, 0.0, faces[3])
                if h == 1:
                    faces[4] = jnp.where(lane == 127, 0.0, faces[4])
                else:
                    faces[5] = jnp.where(lane == 0, 0.0, faces[5])
                for n in range(6):
                    coef[n, p - 1, h] = faces[n] * inverse
                coef[6, p - 1, h] = inverse
                cell = (x * 64 + row) * 256 + 128 * h + lane
                for s in range(2):
                    spot = position[src * 2 + s]
                    drive[p - 1, s, h] = jnp.where(cell == spot, source_gain * inverse, 0.0)
            return carry

        lax.fori_loop(0, count, body, 0)

    def take_in(source, place, low, count):
        def body(i, carry):
            p = low + i
            for s in range(2):
                for h in range(2):
                    place[p, s, h] = slots(source, s, p, h)
            return carry

        lax.fori_loop(0, count, body, 0)

    def sweep(old, new, low, count):
        def body(i, carry):
            p = low + i
            for s in range(2):
                centre = [old[p, s, h] for h in range(2)]
                zn, zp = z_next(centre, False), z_prev(centre, False)
                for h in range(2):
                    mid = centre[h]
                    value = drive[p - 1, s, h] + coef[0, p - 1, h] * old[p + 1, s, h]
                    value = value + coef[1, p - 1, h] * old[p - 1, s, h]
                    value = value + coef[2, p - 1, h] * y_next(mid, False)
                    value = value + coef[3, p - 1, h] * y_prev(mid, False)
                    value = value + coef[4, p - 1, h] * zn[h]
                    value = value + coef[5, p - 1, h] * zp[h]
                    new[p, s, h] = value
            return carry

        lax.fori_loop(0, count, body, 0)

    def pick(even, odd):
        return jnp.where(core == 0, even, odd)

    def early(k):
        return pick(k, k - LOW) + LOW, pick(depth + LOW + 1 - 2 * k, depth + LOW - 2 * k)

    def late(k):
        return pick(k - LOW, depth - k) + LOW, pick(LOW, LOW + 1)

    def solve(fields, part):
        for k in range(1, SWEEPS + 1):
            low, count = part(k)
            sweep(fields[(k - 1) % 2], fields[k % 2], low, count)

    def await_halo(arrays, near):
        for d in range(2):
            on_core = (1 - d) if near else d
            wanted = jnp.logical_and(core == on_core, gets_from[d])

            @pl.when(wanted)
            def _():
                for a in arrays:
                    for h in range(2):
                        halos[a][d][h].wait_recv()

    for which in range(4):
        for h in range(2):
            own[h][which].wait()
    await_halo((0, 1), True)
    near_low = pick(1, 1 - LOW) + LOW
    near_count = pick(depth + LOW - 1, depth + LOW - 2)
    far_low = pick(1 - LOW, depth - 1) + LOW
    far_count = pick(LOW, LOW + 1)
    coefficients(near_low, near_count)
    await_halo((2,), True)
    take_in(fwd_in, field, pick(0, -LOW) + LOW, pick(depth + HIGH, depth + LOW))
    solve((field, other), early)
    await_halo((3,), True)
    take_in(adj_in, adjf, pick(0, -LOW) + LOW, pick(depth + HIGH, depth + LOW))

    identity = jnp.where(
        lax.broadcasted_iota(jnp.int32, (detectors, 128), 0)
        == lax.broadcasted_iota(jnp.int32, (detectors, 128), 1),
        1.0,
        0.0,
    )
    for d in range(2):

        @pl.when(gets_from[d])
        def _():
            det_copy[d].wait_recv()

    for n in range(3):
        where_row = det_in[n] if n < 2 else det_row[...]
        z_row = jnp.broadcast_to((where_row % 256).astype(F32), (8, detectors))
        z_col = lax.dot_general(identity, z_row, NT, precision=HI, preferred_element_type=F32)
        lane = lax.broadcasted_iota(jnp.int32, (detectors, 256), 1).astype(F32)
        zhot[n] = jnp.where(lane == z_col[:, :1], 1.0, 0.0)

    await_halo((0, 1), False)
    coefficients(far_low, far_count)
    await_halo((2,), False)
    take_in(fwd_in, field, pick(-LOW, depth) + LOW, pick(LOW, HIGH))
    solve((field, other), late)

    def gather(d, carry):
        spot = det_scalar[d] - vox * (depth * 64 * 256)
        spot = jnp.clip(spot, 0, depth * 64 * 256 - 1)
        p = spot // (64 * 256)
        y = spot // 256 % 64
        for s in range(2):
            for h in range(2):
                picked[s, h, pl.ds(d, 1), :] = field[p + LOW, s, h, y % 8, pl.ds(y // 8, 1), :]
        return carry

    lax.fori_loop(0, detectors, gather, 0)
    for copy in agg_copy:
        copy.wait()
    sums = agg_in[0]
    for g in range(1, groups):
        sums = sums + agg_in[g]
    predicted = []
    for s in range(2):
        both = picked[s, 0] * zhot[2, :, :128] + picked[s, 1] * zhot[2, :, 128:]
        predicted.append(
            lax.dot_general(
                jnp.ones((8, 128), F32), both, NT, precision=HI, preferred_element_type=F32
            )
        )
    rows8 = lax.broadcasted_iota(jnp.int32, (8, detectors), 0)
    val[...] = sums * jnp.where(rows8 == 0, predicted[0], predicted[1]) - pltpu.roll(sums, 6, 0)
    val_copy = [
        pltpu.make_async_remote_copy(
            src_ref=val,
            dst_ref=val_in.at[d],
            send_sem=val_send.at[d],
            recv_sem=val_recv.at[d],
            device_id=(above, below)[d],
            device_id_type=MESH,
        )
        for d in range(2)
    ]
    for d in range(2):

        @pl.when(sends_to[d])
        def _():
            val_copy[d].start()

    def place_totals(n, totals, where_row, base, low, count):
        spot = where_row - (vox * depth + base) * (64 * 256)
        y = spot // 256 % 64
        code = spot // (64 * 256) * 64 + y % 8 * 8 + y // 8
        parts = [three_parts(totals[s : s + 1]) for s in range(2)]
        hot = zhot[n].astype(BF16)
        hot = jnp.concatenate([hot, hot, hot], axis=0)

        def body(i, carry):
            p = low + i
            rows64 = lax.broadcasted_iota(jnp.int32, (64, detectors), 0) + (p - base) * 64
            match = rows64 == code
            for s in range(2):
                left = [jnp.where(match, part, 0.0).astype(BF16) for part in parts[s]]
                value = lax.dot_general(
                    jnp.concatenate(left, axis=1),
                    hot,
                    (((1,), (0,)), ((), ())),
                    preferred_element_type=F32,
                )
                for h in range(2):
                    half = value[:, 128 * h : 128 * h + 128].reshape(8, 8, 128)
                    drive[p + LOW - 1, s, h] = half * coef[6, p + LOW - 1, h]
            return carry

        lax.fori_loop(0, count, body, 0)

    place_totals(2, val[...], det_row[...], 0, 0, depth)

    def await_values(near):
        for d in range(2):
            on_core = (1 - d) if near else d

            @pl.when(core == on_core)
            def _():
                @pl.when(gets_from[d])
                def _():
                    val_copy[d].wait_recv()

                if d == 0:
                    place_totals(0, val_in[0], det_in[0], -depth, 1 - LOW, LOW - 1)
                else:
                    place_totals(1, val_in[1], det_in[1], depth, depth, HIGH - 1)

    await_values(True)
    solve((adjf, other), early)
    await_values(False)
    await_halo((3,), False)
    take_in(adj_in, adjf, pick(-LOW, depth) + LOW, pick(LOW, HIGH))
    solve((adjf, other), late)

    tile = 64 // groups
    half_depth = depth // 2

    def gradient(i, carry):
        p = i + LOW
        mua_sum = [jnp.zeros((8, 8, 128), F32) for _ in range(2)]
        kap_sum = [jnp.zeros((8, 8, 128), F32) for _ in range(2)]
        for s in range(2):
            f = [field[p, s, h] for h in range(2)]
            a = [adjf[p, s, h] for h in range(2)]
            fz, az = z_next(f, True), z_next(a, True)
            for h in range(2):
                mua_sum[h] = mua_sum[h] - f[h] * a[h]
                product = (field[p + 1, s, h] - f[h]) * (adjf[p + 1, s, h] - a[h])
                product = product + (y_next(f[h], True) - f[h]) * (y_next(a[h], True) - a[h])
                product = product + (fz[h] - f[h]) * (az[h] - a[h])
                kap_sum[h] = kap_sum[h] - product
        for h in range(2):
            for j in range(8):
                grad[0, i, h, pl.ds(j, 8, stride=8), :] = mua_sum[h][j]
                grad[1, i, h, pl.ds(j, 8, stride=8), :] = kap_sum[h][j]
        return carry

    grad_copy = []
    for part in range(2):
        lax.fori_loop(part * half_depth, (part + 1) * half_depth, gradient, 0)
        planes = pl.ds(part * half_depth, half_depth)
        for step, peer in enumerate(peers):
            copy = pltpu.make_async_remote_copy(
                src_ref=grad.at[:, planes, :, pl.ds(pl.multiple_of(tile * peer, 8), tile)],
                dst_ref=grad_in.at[step, :, planes],
                send_sem=grad_send.at[part, step],
                recv_sem=grad_recv.at[part, step],
                device_id={"src": peer},
                device_id_type=MESH,
            )
            copy.start()
            grad_copy.append(copy)

    for d in range(2):

        @pl.when(sends_to[d])
        def _():
            det_copy[d].wait_send()
            val_copy[d].wait_send()
            for a in range(4):
                for h in range(2):
                    halos[a][d][h].wait_send()

    for copy in grad_copy:
        copy.wait()
    mine = pl.ds(pl.multiple_of(tile * src, 8), tile)
    for q, out in ((0, out_mua), (1, out_kappa)):
        for h in range(2):
            value = grad[q, :, h, mine, :]
            for step in range(groups - 1):
                value = value + grad_in[step, q, :, h]
            out[:, :, 128 * h : 128 * h + 128] = value


def body(
    kappa,
    mua,
    prior_forward_fields,
    prior_adjoint_fields,
    source_position,
    detector_voxel,
    measured_source,
    measured_detector,
    measured_data,
    measured_weight,
):
    groups = lax.axis_size("src")
    slabs = lax.axis_size("vox")
    depth, width, _ = kappa.shape
    total = LOW + depth + HIGH
    detectors = detector_voxel.shape[0]
    blocks = (-1, 128)
    hbm = pl.BlockSpec(memory_space=pl.ANY)
    vmem = pl.BlockSpec(memory_space=pltpu.VMEM)
    smem = pl.BlockSpec(memory_space=pltpu.SMEM)
    tile = width // groups
    dma = pltpu.SemaphoreType.DMA
    slab_field = pltpu.VMEM((total, 2, 2, 8, 8, 128), F32)
    return pl.pallas_call(
        functools.partial(kernel, groups, slabs),
        out_shape=(jax.ShapeDtypeStruct((depth, tile, 256), F32),) * 2,
        in_specs=[hbm] * 4 + [smem] * 2 + [vmem] * 5,
        out_specs=(vmem, vmem),
        scratch_shapes=[
            pltpu.VMEM((total, 2, 64, 128), F32),
            pltpu.VMEM((total, 2, 64, 128), F32),
            pltpu.VMEM((2, total, 2, 64, 128), F32),
            pltpu.VMEM((2, total, 2, 64, 128), F32),
            slab_field,
            slab_field,
            slab_field,
            pltpu.VMEM((7, total - 2, 2, 8, 8, 128), F32),
            pltpu.VMEM((total - 2, 2, 2, 8, 8, 128), F32),
            pltpu.VMEM((8 * groups, detectors), F32),
            pltpu.VMEM((groups, 8, detectors), F32),
            pltpu.VMEM((8, detectors), F32),
            pltpu.VMEM((2, 8, detectors), F32),
            pltpu.VMEM((2, 1, detectors), jnp.int32),
            pltpu.VMEM((3, detectors, 256), F32),
            pltpu.VMEM((2, 2, detectors, 128), F32),
            pltpu.VMEM((2, depth, 2, 64, 128), F32),
            pltpu.VMEM((groups - 1, 2, depth, 2, tile, 128), F32),
            dma((4, 2)),
            dma((4, 2, 2)),
            dma((4, 2, 2)),
            dma((2,)),
            dma((2,)),
            dma((groups - 1,)),
            dma((groups - 1,)),
            dma((2,)),
            dma((2,)),
            dma((2, groups - 1)),
            dma((2, groups - 1)),
        ],
        compiler_params=pltpu.CompilerParams(
            collective_id=0, has_side_effects=True, vmem_limit_bytes=60000 * 1024
        ),
        name="tomography",
    )(
        kappa,
        mua,
        prior_forward_fields,
        prior_adjoint_fields,
        source_position,
        detector_voxel,
        detector_voxel.reshape(1, detectors),
        measured_source.reshape(blocks),
        measured_detector.reshape(blocks),
        measured_data.reshape(blocks),
        measured_weight.reshape(blocks),
    )


def solution(mesh):
    in_specs = (
        P("vox", None, None),
        P("vox", None, None),
        P("src", "vox", None, None),
        P("src", "vox", None, None),
        P(),
        P("vox"),
        P(("src", "vox")),
        P(("src", "vox")),
        P(("src", "vox")),
        P(("src", "vox")),
    )
    out_specs = (P("vox", "src", None), P("vox", "src", None))
    return jax.shard_map(body, mesh=mesh, in_specs=in_specs, out_specs=out_specs, check_vma=False)
```

```python
import functools

import jax
import jax.numpy as jnp
from jax import lax
from jax.experimental import pallas as pl
from jax.experimental.pallas import tpu as pltpu
from jax.sharding import PartitionSpec as P

SWEEPS = 6
SHARE = 4
LOW = SWEEPS
HIGH = SWEEPS + 1
source_gain = 10.0

MESH = pl.DeviceIdType.MESH
F32 = jnp.float32
BF16 = jnp.bfloat16
HI = lax.Precision.HIGHEST
NT = (((1,), (1,)), ((), ()))


def slots(ref, *lead):
    return jnp.stack([ref[(*lead, pl.ds(j, 8, stride=8), slice(None))] for j in range(8)])


def y_next(value, zero_edge):
    wrapped = pltpu.roll(value[:1], 7, 1)
    if zero_edge:
        rows = lax.broadcasted_iota(jnp.int32, wrapped.shape, 1)
        wrapped = jnp.where(rows == 7, 0.0, wrapped)
    return jnp.concatenate([value[1:], wrapped], axis=0)


def y_prev(value, zero_edge):
    wrapped = pltpu.roll(value[-1:], 1, 1)
    if zero_edge:
        rows = lax.broadcasted_iota(jnp.int32, wrapped.shape, 1)
        wrapped = jnp.where(rows == 0, 0.0, wrapped)
    return jnp.concatenate([wrapped, value[:-1]], axis=0)


def z_next(halves, zero_edge):
    lane = lax.broadcasted_iota(jnp.int32, halves[0].shape, halves[0].ndim - 1)
    turned = [pltpu.roll(half, 127, half.ndim - 1) for half in halves]
    last = jnp.where(lane == 127, 0.0, turned[1]) if zero_edge else turned[1]
    return [jnp.where(lane == 127, turned[1], turned[0]), last]


def z_prev(halves, zero_edge):
    lane = lax.broadcasted_iota(jnp.int32, halves[0].shape, halves[0].ndim - 1)
    turned = [pltpu.roll(half, 1, half.ndim - 1) for half in halves]
    first = jnp.where(lane == 0, 0.0, turned[0]) if zero_edge else turned[0]
    return [first, jnp.where(lane == 0, turned[0], turned[1])]


def three_parts(value):
    high = value.astype(BF16)
    rest = value - high.astype(F32)
    middle = rest.astype(BF16)
    low = (rest - middle.astype(F32)).astype(BF16)
    return high.astype(F32), middle.astype(F32), low.astype(F32)


def kernel(
    groups,
    slabs,
    kappa,
    mua,
    prior_fwd,
    prior_adj,
    position,
    det_scalar,
    det_row,
    row_source,
    row_detector,
    row_data,
    row_weight,
    out_mua,
    out_kappa,
    kap,
    mu,
    fwd_in,
    adj_in,
    field,
    other,
    adjf,
    coef,
    drive,
    agg,
    agg_in,
    val,
    val_in,
    det_in,
    zhot,
    picked,
    grad,
    grad_in,
    local_sem,
    halo_send,
    halo_recv,
    relay_send,
    relay_recv,
    det_send,
    det_recv,
    agg_send,
    agg_recv,
    val_send,
    val_recv,
    grad_send,
    grad_recv,
):
    src = lax.axis_index("src")
    vox = lax.axis_index("vox")
    core = lax.rem(vox, 2)
    depth = kappa.shape[0]
    total = LOW + depth + HIGH
    detectors = det_row.shape[1]
    has_low = vox > 0
    has_high = vox < slabs - 1
    below = {"vox": jnp.maximum(vox - 1, 0)}
    above = {"vox": jnp.minimum(vox + 1, slabs - 1)}
    peers = [lax.rem(src + step, groups) for step in range(1, groups)]

    barrier = pltpu.get_barrier_semaphore()

    @pl.when(has_high)
    def _():
        pl.semaphore_signal(barrier, inc=1, device_id=above, device_id_type=MESH)

    @pl.when(has_low)
    def _():
        pl.semaphore_signal(barrier, inc=1, device_id=below, device_id_type=MESH)

    for peer in peers:
        pl.semaphore_signal(barrier, inc=1, device_id={"src": peer}, device_id_type=MESH)

    own = []
    for h in range(2):
        lanes = pl.ds(128 * h, 128)
        own.append(
            [
                pltpu.make_async_copy(
                    kappa.at[:, :, lanes], kap.at[pl.ds(LOW, depth), h], local_sem.at[0, h]
                ),
                pltpu.make_async_copy(
                    mua.at[:, :, lanes], mu.at[pl.ds(LOW, depth), h], local_sem.at[1, h]
                ),
                pltpu.make_async_copy(
                    prior_fwd.at[:, :, :, lanes],
                    fwd_in.at[:, pl.ds(LOW, depth), h],
                    local_sem.at[2, h],
                ),
                pltpu.make_async_copy(
                    prior_adj.at[:, :, :, lanes],
                    adj_in.at[:, pl.ds(LOW, depth), h],
                    local_sem.at[3, h],
                ),
            ]
        )
    for which in range(4):
        for h in range(2):
            own[h][which].start()

    pl.semaphore_wait(
        barrier, groups - 1 + jnp.where(has_low, 1, 0) + jnp.where(has_high, 1, 0)
    )

    member = lax.rem(src, SHARE)
    share_rows = 64 // SHARE

    def part_of(who):
        return pl.ds(pl.multiple_of(share_rows * who, 8), share_rows)

    def halo(array, direction, h, far):
        lanes = pl.ds(128 * h, 128)
        rows = part_of(member) if far and array < 2 else pl.ds(0, 64)
        if direction == 0:
            count = LOW - 1 if array == 1 else LOW
            start, target = depth - count, LOW - count
        else:
            count = HIGH - 1 if array == 1 else HIGH
            start, target = 0, LOW + depth
        if array < 2:
            source = (kappa, mua)[array].at[pl.ds(start, count), rows, lanes]
            place = (kap, mu)[array].at[pl.ds(target, count), h, rows]
        else:
            source = (prior_fwd, prior_adj)[array - 2].at[:, pl.ds(start, count), :, lanes]
            place = (fwd_in, adj_in)[array - 2].at[:, pl.ds(target, count), h]
        return pltpu.make_async_remote_copy(
            src_ref=source,
            dst_ref=place,
            send_sem=halo_send.at[array, direction, h],
            recv_sem=halo_recv.at[array, direction, h],
            device_id=above if direction == 0 else below,
            device_id_type=MESH,
        )

    near_halos, far_halos = [
        [[[halo(a, d, h, far) for h in range(2)] for d in range(2)] for a in range(4)]
        for far in (False, True)
    ]
    det_copy = [
        pltpu.make_async_remote_copy(
            src_ref=det_row,
            dst_ref=det_in.at[d],
            send_sem=det_send.at[d],
            recv_sem=det_recv.at[d],
            device_id=(above, below)[d],
            device_id_type=MESH,
        )
        for d in range(2)
    ]

    sends_to = (has_high, has_low)
    gets_from = (has_low, has_high)
    for d in range(2):

        @pl.when(sends_to[d])
        def _():
            det_copy[d].start()

        for far in (False, True):

            @pl.when(jnp.logical_and(sends_to[d], core == (1 - d if far else d)))
            def _():
                for a in range(4):
                    for h in range(2):
                        (near_halos, far_halos)[far][a][d][h].start()

    def relay(array, direction, h, step):
        if direction == 0:
            count = LOW - 1 if array == 1 else LOW
            target = LOW - count
        else:
            count = HIGH - 1 if array == 1 else HIGH
            target = LOW + depth
        place = (kap, mu)[array].at[pl.ds(target, count), h, part_of(member)]
        return pltpu.make_async_remote_copy(
            src_ref=place,
            dst_ref=place,
            send_sem=relay_send.at[array, h, step - 1],
            recv_sem=relay_recv.at[array, h, step - 1],
            device_id={"src": src - member + lax.rem(member + step, SHARE)},
            device_id_type=MESH,
        )

    def relays(direction):
        return [
            relay(a, direction, h, step)
            for a in range(2)
            for h in range(2)
            for step in range(1, SHARE)
        ]

    def far_side(action):
        for d in range(2):

            @pl.when(jnp.logical_and(core == d, gets_from[d]))
            def _():
                action(d)

    for d in range(2):

        @pl.when(jnp.logical_not(gets_from[d]))
        def _():
            if d == 0:
                planes = slice(0, LOW)
            else:
                planes = slice(LOW + depth, total)
            kap[planes] = jnp.zeros_like(kap[planes])
            fwd_in[:, planes] = jnp.zeros_like(fwd_in[:, planes])
            adj_in[:, planes] = jnp.zeros_like(adj_in[:, planes])
            det_in[d] = jnp.zeros_like(det_in[d])
            val_in[d] = jnp.zeros_like(val_in[d])

    rows = lax.broadcasted_iota(jnp.int32, (8 * groups, 128), 0)
    kind = rows % 8
    source_of = rows // 8 * 2 + kind % 2
    det_base = vox * detectors
    det_ids = lax.broadcasted_iota(jnp.int32, (detectors, 128), 0) + det_base
    summed = jnp.zeros((8 * groups, detectors), F32)
    for i in range(row_source.shape[0]):
        weight = row_weight[i : i + 1, :]
        weighted = weight * row_data[i : i + 1, :]
        chosen = jnp.where(kind < 2, weight, jnp.where(kind < 4, weighted, 0.0))
        chosen = jnp.where(row_source[i : i + 1, :] == source_of, chosen, 0.0)
        hot = jnp.where(row_detector[i : i + 1, :] == det_ids, 1.0, 0.0)
        summed = summed + lax.dot_general(
            chosen, hot, NT, precision=HI, preferred_element_type=F32
        )
    agg[...] = summed
    agg_copy = []
    for step, peer in enumerate(peers):
        copy = pltpu.make_async_remote_copy(
            src_ref=agg.at[pl.ds(pl.multiple_of(8 * peer, 8), 8)],
            dst_ref=agg_in.at[src],
            send_sem=agg_send.at[step],
            recv_sem=agg_recv.at[step],
            device_id={"src": peer},
            device_id_type=MESH,
        )
        copy.start()
        agg_copy.append(copy)
    agg_in[src] = agg[pl.ds(pl.multiple_of(8 * src, 8), 8), :]

    def coefficients(low, count):
        def body(i, carry):
            p = low + i
            x = vox * depth + p - LOW
            inside = jnp.logical_and(x >= 0, x < slabs * depth)
            centre = [slots(kap, p, h) for h in range(2)]
            zn, zp = z_next(centre, True), z_prev(centre, True)
            row = lax.broadcasted_iota(jnp.int32, (8, 8, 128), 1) * 8 + lax.broadcasted_iota(
                jnp.int32, (8, 8, 128), 0
            )
            lane = lax.broadcasted_iota(jnp.int32, (8, 8, 128), 2)
            for h in range(2):
                mid = centre[h]
                faces = [
                    0.5 * (slots(kap, p + 1, h) + mid),
                    0.5 * (mid + slots(kap, p - 1, h)),
                    0.5 * (y_next(mid, True) + mid),
                    0.5 * (mid + y_prev(mid, True)),
                    0.5 * (zn[h] + mid),
                    0.5 * (mid + zp[h]),
                ]
                diagonal = slots(mu, p, h)
                for face in faces:
                    diagonal = diagonal + face
                inverse = jnp.where(inside, 1.0 / jnp.where(inside, diagonal, 1.0), 0.0)
                faces[2] = jnp.where(row == 63, 0.0, faces[2])
                faces[3] = jnp.where(row == 0, 0.0, faces[3])
                if h == 1:
                    faces[4] = jnp.where(lane == 127, 0.0, faces[4])
                else:
                    faces[5] = jnp.where(lane == 0, 0.0, faces[5])
                for n in range(6):
                    coef[n, p - 1, h] = faces[n] * inverse
                coef[6, p - 1, h] = inverse
                cell = (x * 64 + row) * 256 + 128 * h + lane
                for s in range(2):
                    spot = position[src * 2 + s]
                    drive[p - 1, s, h] = jnp.where(cell == spot, source_gain * inverse, 0.0)
            return carry

        lax.fori_loop(0, count, body, 0)

    def take_in(source, place, low, count):
        def body(i, carry):
            p = low + i
            for s in range(2):
                for h in range(2):
                    place[p, s, h] = slots(source, s, p, h)
            return carry

        lax.fori_loop(0, count, body, 0)

    def sweep(old, new, low, count):
        def body(i, carry):
            p = low + i
            for s in range(2):
                centre = [old[p, s, h] for h in range(2)]
                zn, zp = z_next(centre, False), z_prev(centre, False)
                for h in range(2):
                    mid = centre[h]
                    value = drive[p - 1, s, h] + coef[0, p - 1, h] * old[p + 1, s, h]
                    value = value + coef[1, p - 1, h] * old[p - 1, s, h]
                    value = value + coef[2, p - 1, h] * y_next(mid, False)
                    value = value + coef[3, p - 1, h] * y_prev(mid, False)
                    value = value + coef[4, p - 1, h] * zn[h]
                    value = value + coef[5, p - 1, h] * zp[h]
                    new[p, s, h] = value
            return carry

        lax.fori_loop(0, count, body, 0)

    def pick(even, odd):
        return jnp.where(core == 0, even, odd)

    def early(k):
        return pick(k, k - LOW) + LOW, pick(depth + LOW + 1 - 2 * k, depth + LOW - 2 * k)

    def late(k):
        return pick(k - LOW, depth - k) + LOW, pick(LOW, LOW + 1)

    def solve(fields, part, first=1, last=SWEEPS):
        for k in range(first, last + 1):
            low, count = part(k)
            sweep(fields[(k - 1) % 2], fields[k % 2], low, count)

    def await_halo(arrays, near):
        for d in range(2):
            on_core = (1 - d) if near else d
            wanted = jnp.logical_and(core == on_core, gets_from[d])

            @pl.when(wanted)
            def _():
                for a in arrays:
                    for h in range(2):
                        (far_halos, near_halos)[near][a][d][h].wait_recv()

    for which in range(4):
        for h in range(2):
            own[h][which].wait()
    await_halo((0, 1), True)
    near_low = pick(1, 1 - LOW) + LOW
    near_count = pick(depth + LOW - 1, depth + LOW - 2)
    far_low = pick(1 - LOW, depth - 1) + LOW
    far_count = pick(LOW, LOW + 1)
    coefficients(near_low, near_count)
    await_halo((2,), True)
    take_in(fwd_in, field, pick(0, -LOW) + LOW, pick(depth + HIGH, depth + LOW))
    solve((field, other), early, 1, 2)

    def pass_on(d):
        for a in range(2):
            for h in range(2):
                far_halos[a][d][h].wait_recv()
        for copy in relays(d):
            copy.start()

    far_side(pass_on)
    solve((field, other), early, 3, SWEEPS)
    await_halo((3,), True)
    take_in(adj_in, adjf, pick(0, -LOW) + LOW, pick(depth + HIGH, depth + LOW))

    identity = jnp.where(
        lax.broadcasted_iota(jnp.int32, (detectors, 128), 0)
        == lax.broadcasted_iota(jnp.int32, (detectors, 128), 1),
        1.0,
        0.0,
    )
    for d in range(2):

        @pl.when(gets_from[d])
        def _():
            det_copy[d].wait_recv()

    for n in range(3):
        where_row = det_in[n] if n < 2 else det_row[...]
        z_row = jnp.broadcast_to((where_row % 256).astype(F32), (8, detectors))
        z_col = lax.dot_general(identity, z_row, NT, precision=HI, preferred_element_type=F32)
        lane = lax.broadcasted_iota(jnp.int32, (detectors, 256), 1).astype(F32)
        zhot[n] = jnp.where(lane == z_col[:, :1], 1.0, 0.0)

    def shared(d):
        for copy in relays(d):
            copy.wait_recv()

    far_side(shared)
    coefficients(far_low, far_count)
    await_halo((2,), False)
    take_in(fwd_in, field, pick(-LOW, depth) + LOW, pick(LOW, HIGH))
    solve((field, other), late)

    def gather(d, carry):
        spot = det_scalar[d] - vox * (depth * 64 * 256)
        spot = jnp.clip(spot, 0, depth * 64 * 256 - 1)
        p = lax.shift_right_logical(spot, 14)
        row = lax.shift_right_logical(spot, 8)
        slot = lax.bitwise_and(row, 7)
        sublane = lax.bitwise_and(lax.shift_right_logical(row, 3), 7)
        for s in range(2):
            for h in range(2):
                picked[s, h, pl.ds(d, 1), :] = field[p + LOW, s, h, slot, pl.ds(sublane, 1), :]
        return carry

    lax.fori_loop(0, detectors, gather, 0, unroll=4)
    for copy in agg_copy:
        copy.wait()
    sums = agg_in[0]
    for g in range(1, groups):
        sums = sums + agg_in[g]
    predicted = []
    for s in range(2):
        both = picked[s, 0] * zhot[2, :, :128] + picked[s, 1] * zhot[2, :, 128:]
        predicted.append(
            lax.dot_general(
                jnp.ones((8, 128), F32), both, NT, precision=HI, preferred_element_type=F32
            )
        )
    rows8 = lax.broadcasted_iota(jnp.int32, (8, detectors), 0)
    val[...] = sums * jnp.where(rows8 == 0, predicted[0], predicted[1]) - pltpu.roll(sums, 6, 0)
    val_copy = [
        pltpu.make_async_remote_copy(
            src_ref=val,
            dst_ref=val_in.at[d],
            send_sem=val_send.at[d],
            recv_sem=val_recv.at[d],
            device_id=(above, below)[d],
            device_id_type=MESH,
        )
        for d in range(2)
    ]
    for d in range(2):

        @pl.when(sends_to[d])
        def _():
            val_copy[d].start()

    def place_totals(n, totals, where_row, base, low, count):
        spot = where_row - (vox * depth + base) * (64 * 256)
        y = spot // 256 % 64
        code = spot // (64 * 256) * 64 + y % 8 * 8 + y // 8
        parts = [three_parts(totals[s : s + 1]) for s in range(2)]
        hot = zhot[n].astype(BF16)
        hot = jnp.concatenate([hot, hot, hot], axis=0)

        def body(i, carry):
            p = low + i
            rows64 = lax.broadcasted_iota(jnp.int32, (64, detectors), 0) + (p - base) * 64
            match = rows64 == code
            for s in range(2):
                left = [jnp.where(match, part, 0.0).astype(BF16) for part in parts[s]]
                value = lax.dot_general(
                    jnp.concatenate(left, axis=1),
                    hot,
                    (((1,), (0,)), ((), ())),
                    preferred_element_type=F32,
                )
                for h in range(2):
                    half = value[:, 128 * h : 128 * h + 128].reshape(8, 8, 128)
                    drive[p + LOW - 1, s, h] = half * coef[6, p + LOW - 1, h]
            return carry

        lax.fori_loop(0, count, body, 0)

    place_totals(2, val[...], det_row[...], 0, 0, depth)

    def await_values(near):
        for d in range(2):
            on_core = (1 - d) if near else d

            @pl.when(core == on_core)
            def _():
                @pl.when(gets_from[d])
                def _():
                    val_copy[d].wait_recv()

                if d == 0:
                    place_totals(0, val_in[0], det_in[0], -depth, 1 - LOW, LOW - 1)
                else:
                    place_totals(1, val_in[1], det_in[1], depth, depth, HIGH - 1)

    await_values(True)
    solve((adjf, other), early)
    await_values(False)
    await_halo((3,), False)
    take_in(adj_in, adjf, pick(-LOW, depth) + LOW, pick(LOW, HIGH))

    def stage(j):
        if j == 0:
            return lambda k: (pick(k, depth - k) + LOW, pick(0, 1))
        return lambda k: (pick(k - 2 * j, depth - 1 - k + 2 * j) + LOW, 2)

    tile = 64 // groups

    def gradient(i, carry):
        p = i + LOW
        mua_sum = [jnp.zeros((8, 8, 128), F32) for _ in range(2)]
        kap_sum = [jnp.zeros((8, 8, 128), F32) for _ in range(2)]
        for s in range(2):
            f = [field[p, s, h] for h in range(2)]
            a = [adjf[p, s, h] for h in range(2)]
            fz, az = z_next(f, True), z_next(a, True)
            for h in range(2):
                mua_sum[h] = mua_sum[h] - f[h] * a[h]
                product = (field[p + 1, s, h] - f[h]) * (adjf[p + 1, s, h] - a[h])
                product = product + (y_next(f[h], True) - f[h]) * (y_next(a[h], True) - a[h])
                product = product + (fz[h] - f[h]) * (az[h] - a[h])
                kap_sum[h] = kap_sum[h] - product
        for h in range(2):
            for j in range(8):
                grad[0, i, h, pl.ds(j, 8, stride=8), :] = mua_sum[h][j]
                grad[1, i, h, pl.ds(j, 8, stride=8), :] = kap_sum[h][j]
        return carry

    grad_copy = []
    for part in range(depth // 2):
        solve((adjf, other), stage(part))
        first = pick(depth - 2 - 2 * part, 2 * part)
        lax.fori_loop(first, first + 2, gradient, 0)
        planes = pl.ds(first, 2)
        for step, peer in enumerate(peers):
            copy = pltpu.make_async_remote_copy(
                src_ref=grad.at[:, planes, :, pl.ds(pl.multiple_of(tile * peer, 8), tile)],
                dst_ref=grad_in.at[step, :, planes],
                send_sem=grad_send.at[part, step],
                recv_sem=grad_recv.at[part, step],
                device_id={"src": peer},
                device_id_type=MESH,
            )
            copy.start()
            grad_copy.append(copy)

    for d in range(2):

        @pl.when(sends_to[d])
        def _():
            det_copy[d].wait_send()
            val_copy[d].wait_send()

        for far in (False, True):

            @pl.when(jnp.logical_and(sends_to[d], core == (1 - d if far else d)))
            def _():
                for a in range(4):
                    for h in range(2):
                        (near_halos, far_halos)[far][a][d][h].wait_send()

    def relays_left(d):
        for copy in relays(d):
            copy.wait_send()

    far_side(relays_left)

    for copy in grad_copy:
        copy.wait()
    mine = pl.ds(pl.multiple_of(tile * src, 8), tile)
    for q, out in ((0, out_mua), (1, out_kappa)):
        for h in range(2):
            value = grad[q, :, h, mine, :]
            for step in range(groups - 1):
                value = value + grad_in[step, q, :, h]
            out[:, :, 128 * h : 128 * h + 128] = value


def body(
    kappa,
    mua,
    prior_forward_fields,
    prior_adjoint_fields,
    source_position,
    detector_voxel,
    measured_source,
    measured_detector,
    measured_data,
    measured_weight,
):
    groups = lax.axis_size("src")
    slabs = lax.axis_size("vox")
    depth, width, _ = kappa.shape
    total = LOW + depth + HIGH
    detectors = detector_voxel.shape[0]
    blocks = (-1, 128)
    hbm = pl.BlockSpec(memory_space=pl.ANY)
    vmem = pl.BlockSpec(memory_space=pltpu.VMEM)
    smem = pl.BlockSpec(memory_space=pltpu.SMEM)
    tile = width // groups
    dma = pltpu.SemaphoreType.DMA
    slab_field = pltpu.VMEM((total, 2, 2, 8, 8, 128), F32)
    return pl.pallas_call(
        functools.partial(kernel, groups, slabs),
        out_shape=(jax.ShapeDtypeStruct((depth, tile, 256), F32),) * 2,
        in_specs=[hbm] * 4 + [smem] * 2 + [vmem] * 5,
        out_specs=(vmem, vmem),
        scratch_shapes=[
            pltpu.VMEM((total, 2, 64, 128), F32),
            pltpu.VMEM((total, 2, 64, 128), F32),
            pltpu.VMEM((2, total, 2, 64, 128), F32),
            pltpu.VMEM((2, total, 2, 64, 128), F32),
            slab_field,
            slab_field,
            slab_field,
            pltpu.VMEM((7, total - 2, 2, 8, 8, 128), F32),
            pltpu.VMEM((total - 2, 2, 2, 8, 8, 128), F32),
            pltpu.VMEM((8 * groups, detectors), F32),
            pltpu.VMEM((groups, 8, detectors), F32),
            pltpu.VMEM((8, detectors), F32),
            pltpu.VMEM((2, 8, detectors), F32),
            pltpu.VMEM((2, 1, detectors), jnp.int32),
            pltpu.VMEM((3, detectors, 256), F32),
            pltpu.VMEM((2, 2, detectors, 128), F32),
            pltpu.VMEM((2, depth, 2, 64, 128), F32),
            pltpu.VMEM((groups - 1, 2, depth, 2, tile, 128), F32),
            dma((4, 2)),
            dma((4, 2, 2)),
            dma((4, 2, 2)),
            dma((2, 2, SHARE - 1)),
            dma((2, 2, SHARE - 1)),
            dma((2,)),
            dma((2,)),
            dma((groups - 1,)),
            dma((groups - 1,)),
            dma((2,)),
            dma((2,)),
            dma((depth // 2, groups - 1)),
            dma((depth // 2, groups - 1)),
        ],
        compiler_params=pltpu.CompilerParams(
            collective_id=0, has_side_effects=True, vmem_limit_bytes=60000 * 1024
        ),
        name="tomography",
    )(
        kappa,
        mua,
        prior_forward_fields,
        prior_adjoint_fields,
        source_position,
        detector_voxel,
        detector_voxel.reshape(1, detectors),
        measured_source.reshape(blocks),
        measured_detector.reshape(blocks),
        measured_data.reshape(blocks),
        measured_weight.reshape(blocks),
    )


def solution(mesh):
    in_specs = (
        P("vox", None, None),
        P("vox", None, None),
        P("src", "vox", None, None),
        P("src", "vox", None, None),
        P(),
        P("vox"),
        P(("src", "vox")),
        P(("src", "vox")),
        P(("src", "vox")),
        P(("src", "vox")),
    )
    out_specs = (P("vox", "src", None), P("vox", "src", None))
    return jax.shard_map(body, mesh=mesh, in_specs=in_specs, out_specs=out_specs, check_vma=False)
```

```python
import functools

import jax
import jax.numpy as jnp
from jax import lax
from jax.experimental import pallas as pl
from jax.experimental.pallas import tpu as pltpu
from jax.sharding import PartitionSpec as P

SWEEPS = 6
LOW = SWEEPS
HIGH = SWEEPS + 1
source_gain = 10.0

MESH = pl.DeviceIdType.MESH
F32 = jnp.float32
BF16 = jnp.bfloat16
HI = lax.Precision.HIGHEST
NT = (((1,), (1,)), ((), ()))


def slots(ref, *lead):
    return jnp.stack([ref[(*lead, pl.ds(j, 8, stride=8), slice(None))] for j in range(8)])


def y_next(value, zero_edge):
    wrapped = pltpu.roll(value[:1], 7, 1)
    if zero_edge:
        rows = lax.broadcasted_iota(jnp.int32, wrapped.shape, 1)
        wrapped = jnp.where(rows == 7, 0.0, wrapped)
    return jnp.concatenate([value[1:], wrapped], axis=0)


def y_prev(value, zero_edge):
    wrapped = pltpu.roll(value[-1:], 1, 1)
    if zero_edge:
        rows = lax.broadcasted_iota(jnp.int32, wrapped.shape, 1)
        wrapped = jnp.where(rows == 0, 0.0, wrapped)
    return jnp.concatenate([wrapped, value[:-1]], axis=0)


def z_next(halves, zero_edge):
    lane = lax.broadcasted_iota(jnp.int32, halves[0].shape, halves[0].ndim - 1)
    turned = [pltpu.roll(half, 127, half.ndim - 1) for half in halves]
    last = jnp.where(lane == 127, 0.0, turned[1]) if zero_edge else turned[1]
    return [jnp.where(lane == 127, turned[1], turned[0]), last]


def z_prev(halves, zero_edge):
    lane = lax.broadcasted_iota(jnp.int32, halves[0].shape, halves[0].ndim - 1)
    turned = [pltpu.roll(half, 1, half.ndim - 1) for half in halves]
    first = jnp.where(lane == 0, 0.0, turned[0]) if zero_edge else turned[0]
    return [first, jnp.where(lane == 0, turned[0], turned[1])]


def three_parts(value):
    high = value.astype(BF16)
    rest = value - high.astype(F32)
    middle = rest.astype(BF16)
    low = (rest - middle.astype(F32)).astype(BF16)
    return high.astype(F32), middle.astype(F32), low.astype(F32)


def kernel(
    groups,
    slabs,
    kappa,
    mua,
    prior_fwd,
    prior_adj,
    position,
    det_scalar,
    det_row,
    row_source,
    row_detector,
    row_data,
    row_weight,
    out_mua,
    out_kappa,
    kap,
    mu,
    fwd_in,
    adj_in,
    field,
    other,
    adjf,
    coef,
    drive,
    agg,
    agg_in,
    val,
    val_in,
    det_in,
    zhot,
    picked,
    grad,
    grad_in,
    local_sem,
    halo_send,
    halo_recv,
    det_send,
    det_recv,
    agg_send,
    agg_recv,
    val_send,
    val_recv,
    grad_send,
    grad_recv,
):
    src = lax.axis_index("src")
    vox = lax.axis_index("vox")
    core = lax.rem(vox, 2)
    depth = kappa.shape[0]
    total = LOW + depth + HIGH
    detectors = det_row.shape[1]
    has_low = vox > 0
    has_high = vox < slabs - 1
    below = {"vox": jnp.maximum(vox - 1, 0)}
    above = {"vox": jnp.minimum(vox + 1, slabs - 1)}
    peers = [lax.rem(src + step, groups) for step in range(1, groups)]

    barrier = pltpu.get_barrier_semaphore()

    @pl.when(has_high)
    def _():
        pl.semaphore_signal(barrier, inc=1, device_id=above, device_id_type=MESH)

    @pl.when(has_low)
    def _():
        pl.semaphore_signal(barrier, inc=1, device_id=below, device_id_type=MESH)

    for peer in peers:
        pl.semaphore_signal(barrier, inc=1, device_id={"src": peer}, device_id_type=MESH)

    own = []
    for h in range(2):
        lanes = pl.ds(128 * h, 128)
        own.append(
            [
                pltpu.make_async_copy(
                    kappa.at[:, :, lanes], kap.at[pl.ds(LOW, depth), h], local_sem.at[0, h]
                ),
                pltpu.make_async_copy(
                    mua.at[:, :, lanes], mu.at[pl.ds(LOW, depth), h], local_sem.at[1, h]
                ),
                pltpu.make_async_copy(
                    prior_fwd.at[:, :, :, lanes],
                    fwd_in.at[:, pl.ds(LOW, depth), h],
                    local_sem.at[2, h],
                ),
                pltpu.make_async_copy(
                    prior_adj.at[:, :, :, lanes],
                    adj_in.at[:, pl.ds(LOW, depth), h],
                    local_sem.at[3, h],
                ),
            ]
        )
    for which in range(4):
        for h in range(2):
            own[h][which].start()

    pl.semaphore_wait(
        barrier, groups - 1 + jnp.where(has_low, 1, 0) + jnp.where(has_high, 1, 0)
    )

    def halo(array, direction, h):
        lanes = pl.ds(128 * h, 128)
        if direction == 0:
            count = LOW - 1 if array == 1 else LOW
            start, target = depth - count, LOW - count
        else:
            count = HIGH - 1 if array == 1 else HIGH
            start, target = 0, LOW + depth
        if array < 2:
            source = (kappa, mua)[array].at[pl.ds(start, count), :, lanes]
            place = (kap, mu)[array].at[pl.ds(target, count), h]
        else:
            source = (prior_fwd, prior_adj)[array - 2].at[:, pl.ds(start, count), :, lanes]
            place = (fwd_in, adj_in)[array - 2].at[:, pl.ds(target, count), h]
        return pltpu.make_async_remote_copy(
            src_ref=source,
            dst_ref=place,
            send_sem=halo_send.at[array, direction, h],
            recv_sem=halo_recv.at[array, direction, h],
            device_id=above if direction == 0 else below,
            device_id_type=MESH,
        )

    halos = [[[halo(a, d, h) for h in range(2)] for d in range(2)] for a in range(4)]
    det_copy = [
        pltpu.make_async_remote_copy(
            src_ref=det_row,
            dst_ref=det_in.at[d],
            send_sem=det_send.at[d],
            recv_sem=det_recv.at[d],
            device_id=(above, below)[d],
            device_id_type=MESH,
        )
        for d in range(2)
    ]

    sends_to = (has_high, has_low)
    gets_from = (has_low, has_high)
    for d in range(2):

        @pl.when(sends_to[d])
        def _():
            det_copy[d].start()
            for a in range(4):
                for h in range(2):
                    halos[a][d][h].start()

    for d in range(2):

        @pl.when(jnp.logical_not(gets_from[d]))
        def _():
            if d == 0:
                planes = slice(0, LOW)
            else:
                planes = slice(LOW + depth, total)
            kap[planes] = jnp.zeros_like(kap[planes])
            fwd_in[:, planes] = jnp.zeros_like(fwd_in[:, planes])
            adj_in[:, planes] = jnp.zeros_like(adj_in[:, planes])
            det_in[d] = jnp.zeros_like(det_in[d])
            val_in[d] = jnp.zeros_like(val_in[d])

    rows = lax.broadcasted_iota(jnp.int32, (8 * groups, 128), 0)
    kind = rows % 8
    source_of = rows // 8 * 2 + kind % 2
    det_base = vox * detectors
    det_ids = lax.broadcasted_iota(jnp.int32, (detectors, 128), 0) + det_base
    summed = jnp.zeros((8 * groups, detectors), F32)
    for i in range(row_source.shape[0]):
        weight = row_weight[i : i + 1, :]
        weighted = weight * row_data[i : i + 1, :]
        chosen = jnp.where(kind < 2, weight, jnp.where(kind < 4, weighted, 0.0))
        chosen = jnp.where(row_source[i : i + 1, :] == source_of, chosen, 0.0)
        hot = jnp.where(row_detector[i : i + 1, :] == det_ids, 1.0, 0.0)
        summed = summed + lax.dot_general(
            chosen, hot, NT, precision=HI, preferred_element_type=F32
        )
    agg[...] = summed
    agg_copy = []
    for step, peer in enumerate(peers):
        copy = pltpu.make_async_remote_copy(
            src_ref=agg.at[pl.ds(pl.multiple_of(8 * peer, 8), 8)],
            dst_ref=agg_in.at[src],
            send_sem=agg_send.at[step],
            recv_sem=agg_recv.at[step],
            device_id={"src": peer},
            device_id_type=MESH,
        )
        copy.start()
        agg_copy.append(copy)
    agg_in[src] = agg[pl.ds(pl.multiple_of(8 * src, 8), 8), :]

    def coefficients(low, count):
        def body(i, carry):
            p = low + i
            x = vox * depth + p - LOW
            inside = jnp.logical_and(x >= 0, x < slabs * depth)
            centre = [slots(kap, p, h) for h in range(2)]
            zn, zp = z_next(centre, True), z_prev(centre, True)
            row = lax.broadcasted_iota(jnp.int32, (8, 8, 128), 1) * 8 + lax.broadcasted_iota(
                jnp.int32, (8, 8, 128), 0
            )
            lane = lax.broadcasted_iota(jnp.int32, (8, 8, 128), 2)
            for h in range(2):
                mid = centre[h]
                faces = [
                    0.5 * (slots(kap, p + 1, h) + mid),
                    0.5 * (mid + slots(kap, p - 1, h)),
                    0.5 * (y_next(mid, True) + mid),
                    0.5 * (mid + y_prev(mid, True)),
                    0.5 * (zn[h] + mid),
                    0.5 * (mid + zp[h]),
                ]
                diagonal = slots(mu, p, h)
                for face in faces:
                    diagonal = diagonal + face
                inverse = jnp.where(inside, 1.0 / jnp.where(inside, diagonal, 1.0), 0.0)
                faces[2] = jnp.where(row == 63, 0.0, faces[2])
                faces[3] = jnp.where(row == 0, 0.0, faces[3])
                if h == 1:
                    faces[4] = jnp.where(lane == 127, 0.0, faces[4])
                else:
                    faces[5] = jnp.where(lane == 0, 0.0, faces[5])
                for n in range(6):
                    coef[n, p - 1, h] = faces[n] * inverse
                coef[6, p - 1, h] = inverse
                cell = (x * 64 + row) * 256 + 128 * h + lane
                for s in range(2):
                    spot = position[src * 2 + s]
                    drive[p - 1, s, h] = jnp.where(cell == spot, source_gain * inverse, 0.0)
            return carry

        lax.fori_loop(0, count, body, 0)

    def take_in(source, place, low, count):
        def body(i, carry):
            p = low + i
            for s in range(2):
                for h in range(2):
                    place[p, s, h] = slots(source, s, p, h)
            return carry

        lax.fori_loop(0, count, body, 0)

    def sweep(old, new, low, count):
        def body(i, carry):
            p = low + i
            for s in range(2):
                centre = [old[p, s, h] for h in range(2)]
                zn, zp = z_next(centre, False), z_prev(centre, False)
                for h in range(2):
                    mid = centre[h]
                    value = drive[p - 1, s, h] + coef[0, p - 1, h] * old[p + 1, s, h]
                    value = value + coef[1, p - 1, h] * old[p - 1, s, h]
                    value = value + coef[2, p - 1, h] * y_next(mid, False)
                    value = value + coef[3, p - 1, h] * y_prev(mid, False)
                    value = value + coef[4, p - 1, h] * zn[h]
                    value = value + coef[5, p - 1, h] * zp[h]
                    new[p, s, h] = value
            return carry

        lax.fori_loop(0, count, body, 0)

    def pick(even, odd):
        return jnp.where(core == 0, even, odd)

    def early(k):
        return pick(k, k - LOW) + LOW, pick(depth + LOW + 1 - 2 * k, depth + LOW - 2 * k)

    def late(k):
        return pick(k - LOW, depth - k) + LOW, pick(LOW, LOW + 1)

    def solve(fields, part):
        for k in range(1, SWEEPS + 1):
            low, count = part(k)
            sweep(fields[(k - 1) % 2], fields[k % 2], low, count)

    def await_halo(arrays, near):
        for d in range(2):
            on_core = (1 - d) if near else d
            wanted = jnp.logical_and(core == on_core, gets_from[d])

            @pl.when(wanted)
            def _():
                for a in arrays:
                    for h in range(2):
                        halos[a][d][h].wait_recv()

    for which in range(4):
        for h in range(2):
            own[h][which].wait()
    await_halo((0, 1), True)
    near_low = pick(1, 1 - LOW) + LOW
    near_count = pick(depth + LOW - 1, depth + LOW - 2)
    far_low = pick(1 - LOW, depth - 1) + LOW
    far_count = pick(LOW, LOW + 1)
    coefficients(near_low, near_count)
    await_halo((2,), True)
    take_in(fwd_in, field, pick(0, -LOW) + LOW, pick(depth + HIGH, depth + LOW))
    solve((field, other), early)
    await_halo((3,), True)
    take_in(adj_in, adjf, pick(0, -LOW) + LOW, pick(depth + HIGH, depth + LOW))

    identity = jnp.where(
        lax.broadcasted_iota(jnp.int32, (detectors, 128), 0)
        == lax.broadcasted_iota(jnp.int32, (detectors, 128), 1),
        1.0,
        0.0,
    )
    for d in range(2):

        @pl.when(gets_from[d])
        def _():
            det_copy[d].wait_recv()

    for n in range(3):
        where_row = det_in[n] if n < 2 else det_row[...]
        z_row = jnp.broadcast_to((where_row % 256).astype(F32), (8, detectors))
        z_col = lax.dot_general(identity, z_row, NT, precision=HI, preferred_element_type=F32)
        lane = lax.broadcasted_iota(jnp.int32, (detectors, 256), 1).astype(F32)
        zhot[n] = jnp.where(lane == z_col[:, :1], 1.0, 0.0)

    await_halo((0, 1), False)
    coefficients(far_low, far_count)
    await_halo((2,), False)
    take_in(fwd_in, field, pick(-LOW, depth) + LOW, pick(LOW, HIGH))
    solve((field, other), late)

    def gather(d, carry):
        spot = det_scalar[d] - vox * (depth * 64 * 256)
        spot = jnp.clip(spot, 0, depth * 64 * 256 - 1)
        p = lax.shift_right_logical(spot, 14)
        row = lax.shift_right_logical(spot, 8)
        slot = lax.bitwise_and(row, 7)
        sublane = lax.bitwise_and(lax.shift_right_logical(row, 3), 7)
        for s in range(2):
            for h in range(2):
                picked[s, h, pl.ds(d, 1), :] = field[p + LOW, s, h, slot, pl.ds(sublane, 1), :]
        return carry

    lax.fori_loop(0, detectors, gather, 0, unroll=4)
    for copy in agg_copy:
        copy.wait()
    sums = agg_in[0]
    for g in range(1, groups):
        sums = sums + agg_in[g]
    predicted = []
    for s in range(2):
        both = picked[s, 0] * zhot[2, :, :128] + picked[s, 1] * zhot[2, :, 128:]
        predicted.append(
            lax.dot_general(
                jnp.ones((8, 128), F32), both, NT, precision=HI, preferred_element_type=F32
            )
        )
    rows8 = lax.broadcasted_iota(jnp.int32, (8, detectors), 0)
    val[...] = sums * jnp.where(rows8 == 0, predicted[0], predicted[1]) - pltpu.roll(sums, 6, 0)
    val_copy = [
        pltpu.make_async_remote_copy(
            src_ref=val,
            dst_ref=val_in.at[d],
            send_sem=val_send.at[d],
            recv_sem=val_recv.at[d],
            device_id=(above, below)[d],
            device_id_type=MESH,
        )
        for d in range(2)
    ]
    for d in range(2):

        @pl.when(sends_to[d])
        def _():
            val_copy[d].start()

    def place_totals(n, totals, where_row, base, low, count):
        spot = where_row - (vox * depth + base) * (64 * 256)
        y = spot // 256 % 64
        code = spot // (64 * 256) * 64 + y % 8 * 8 + y // 8
        parts = [three_parts(totals[s : s + 1]) for s in range(2)]
        hot = zhot[n].astype(BF16)
        hot = jnp.concatenate([hot, hot, hot], axis=0)

        def body(i, carry):
            p = low + i
            rows64 = lax.broadcasted_iota(jnp.int32, (64, detectors), 0) + (p - base) * 64
            match = rows64 == code
            for s in range(2):
                left = [jnp.where(match, part, 0.0).astype(BF16) for part in parts[s]]
                value = lax.dot_general(
                    jnp.concatenate(left, axis=1),
                    hot,
                    (((1,), (0,)), ((), ())),
                    preferred_element_type=F32,
                )
                for h in range(2):
                    half = value[:, 128 * h : 128 * h + 128].reshape(8, 8, 128)
                    drive[p + LOW - 1, s, h] = half * coef[6, p + LOW - 1, h]
            return carry

        lax.fori_loop(0, count, body, 0)

    place_totals(2, val[...], det_row[...], 0, 0, depth)

    def await_values(near):
        for d in range(2):
            on_core = (1 - d) if near else d

            @pl.when(core == on_core)
            def _():
                @pl.when(gets_from[d])
                def _():
                    val_copy[d].wait_recv()

                if d == 0:
                    place_totals(0, val_in[0], det_in[0], -depth, 1 - LOW, LOW - 1)
                else:
                    place_totals(1, val_in[1], det_in[1], depth, depth, HIGH - 1)

    await_values(True)
    solve((adjf, other), early)
    await_values(False)
    await_halo((3,), False)
    take_in(adj_in, adjf, pick(-LOW, depth) + LOW, pick(LOW, HIGH))

    def stage(j):
        if j == 0:
            return lambda k: (pick(k, depth - k) + LOW, pick(0, 1))
        return lambda k: (pick(k - 2 * j, depth - 1 - k + 2 * j) + LOW, 2)

    tile = 64 // groups

    def gradient(i, carry):
        p = i + LOW
        mua_sum = [jnp.zeros((8, 8, 128), F32) for _ in range(2)]
        kap_sum = [jnp.zeros((8, 8, 128), F32) for _ in range(2)]
        for s in range(2):
            f = [field[p, s, h] for h in range(2)]
            a = [adjf[p, s, h] for h in range(2)]
            fz, az = z_next(f, True), z_next(a, True)
            for h in range(2):
                mua_sum[h] = mua_sum[h] - f[h] * a[h]
                product = (field[p + 1, s, h] - f[h]) * (adjf[p + 1, s, h] - a[h])
                product = product + (y_next(f[h], True) - f[h]) * (y_next(a[h], True) - a[h])
                product = product + (fz[h] - f[h]) * (az[h] - a[h])
                kap_sum[h] = kap_sum[h] - product
        for h in range(2):
            for j in range(8):
                grad[0, i, h, pl.ds(j, 8, stride=8), :] = mua_sum[h][j]
                grad[1, i, h, pl.ds(j, 8, stride=8), :] = kap_sum[h][j]
        return carry

    grad_copy = []
    for part in range(depth // 2):
        solve((adjf, other), stage(part))
        first = pick(depth - 2 - 2 * part, 2 * part)
        lax.fori_loop(first, first + 2, gradient, 0)
        planes = pl.ds(first, 2)
        for step, peer in enumerate(peers):
            copy = pltpu.make_async_remote_copy(
                src_ref=grad.at[:, planes, :, pl.ds(pl.multiple_of(tile * peer, 8), tile)],
                dst_ref=grad_in.at[step, :, planes],
                send_sem=grad_send.at[part, step],
                recv_sem=grad_recv.at[part, step],
                device_id={"src": peer},
                device_id_type=MESH,
            )
            copy.start()
            grad_copy.append(copy)

    for d in range(2):

        @pl.when(sends_to[d])
        def _():
            det_copy[d].wait_send()
            val_copy[d].wait_send()
            for a in range(4):
                for h in range(2):
                    halos[a][d][h].wait_send()

    for copy in grad_copy:
        copy.wait()
    mine = pl.ds(pl.multiple_of(tile * src, 8), tile)
    for q, out in ((0, out_mua), (1, out_kappa)):
        for h in range(2):
            value = grad[q, :, h, mine, :]
            for step in range(groups - 1):
                value = value + grad_in[step, q, :, h]
            out[:, :, 128 * h : 128 * h + 128] = value


def body(
    kappa,
    mua,
    prior_forward_fields,
    prior_adjoint_fields,
    source_position,
    detector_voxel,
    measured_source,
    measured_detector,
    measured_data,
    measured_weight,
):
    groups = lax.axis_size("src")
    slabs = lax.axis_size("vox")
    depth, width, _ = kappa.shape
    total = LOW + depth + HIGH
    detectors = detector_voxel.shape[0]
    blocks = (-1, 128)
    hbm = pl.BlockSpec(memory_space=pl.ANY)
    vmem = pl.BlockSpec(memory_space=pltpu.VMEM)
    smem = pl.BlockSpec(memory_space=pltpu.SMEM)
    tile = width // groups
    dma = pltpu.SemaphoreType.DMA
    slab_field = pltpu.VMEM((total, 2, 2, 8, 8, 128), F32)
    return pl.pallas_call(
        functools.partial(kernel, groups, slabs),
        out_shape=(jax.ShapeDtypeStruct((depth, tile, 256), F32),) * 2,
        in_specs=[hbm] * 4 + [smem] * 2 + [vmem] * 5,
        out_specs=(vmem, vmem),
        scratch_shapes=[
            pltpu.VMEM((total, 2, 64, 128), F32),
            pltpu.VMEM((total, 2, 64, 128), F32),
            pltpu.VMEM((2, total, 2, 64, 128), F32),
            pltpu.VMEM((2, total, 2, 64, 128), F32),
            slab_field,
            slab_field,
            slab_field,
            pltpu.VMEM((7, total - 2, 2, 8, 8, 128), F32),
            pltpu.VMEM((total - 2, 2, 2, 8, 8, 128), F32),
            pltpu.VMEM((8 * groups, detectors), F32),
            pltpu.VMEM((groups, 8, detectors), F32),
            pltpu.VMEM((8, detectors), F32),
            pltpu.VMEM((2, 8, detectors), F32),
            pltpu.VMEM((2, 1, detectors), jnp.int32),
            pltpu.VMEM((3, detectors, 256), F32),
            pltpu.VMEM((2, 2, detectors, 128), F32),
            pltpu.VMEM((2, depth, 2, 64, 128), F32),
            pltpu.VMEM((groups - 1, 2, depth, 2, tile, 128), F32),
            dma((4, 2)),
            dma((4, 2, 2)),
            dma((4, 2, 2)),
            dma((2,)),
            dma((2,)),
            dma((groups - 1,)),
            dma((groups - 1,)),
            dma((2,)),
            dma((2,)),
            dma((depth // 2, groups - 1)),
            dma((depth // 2, groups - 1)),
        ],
        compiler_params=pltpu.CompilerParams(
            collective_id=0, has_side_effects=True, vmem_limit_bytes=60000 * 1024
        ),
        name="tomography",
    )(
        kappa,
        mua,
        prior_forward_fields,
        prior_adjoint_fields,
        source_position,
        detector_voxel,
        detector_voxel.reshape(1, detectors),
        measured_source.reshape(blocks),
        measured_detector.reshape(blocks),
        measured_data.reshape(blocks),
        measured_weight.reshape(blocks),
    )


def solution(mesh):
    in_specs = (
        P("vox", None, None),
        P("vox", None, None),
        P("src", "vox", None, None),
        P("src", "vox", None, None),
        P(),
        P("vox"),
        P(("src", "vox")),
        P(("src", "vox")),
        P(("src", "vox")),
        P(("src", "vox")),
    )
    out_specs = (P("vox", "src", None), P("vox", "src", None))
    return jax.shard_map(body, mesh=mesh, in_specs=in_specs, out_specs=out_specs, check_vma=False)
```

```python
import functools

import jax
import jax.numpy as jnp
from jax import lax
from jax.experimental import pallas as pl
from jax.experimental.pallas import tpu as pltpu
from jax.sharding import PartitionSpec as P

SWEEPS = 6
LOW = SWEEPS
HIGH = SWEEPS + 1
source_gain = 10.0

MESH = pl.DeviceIdType.MESH
F32 = jnp.float32
BF16 = jnp.bfloat16
HI = lax.Precision.HIGHEST
NT = (((1,), (1,)), ((), ()))


def slots(ref, *lead):
    return jnp.stack([ref[(*lead, pl.ds(j, 8, stride=8), slice(None))] for j in range(8)])


def y_next(value, zero_edge):
    wrapped = pltpu.roll(value[:1], 7, 1)
    if zero_edge:
        rows = lax.broadcasted_iota(jnp.int32, wrapped.shape, 1)
        wrapped = jnp.where(rows == 7, 0.0, wrapped)
    return jnp.concatenate([value[1:], wrapped], axis=0)


def y_prev(value, zero_edge):
    wrapped = pltpu.roll(value[-1:], 1, 1)
    if zero_edge:
        rows = lax.broadcasted_iota(jnp.int32, wrapped.shape, 1)
        wrapped = jnp.where(rows == 0, 0.0, wrapped)
    return jnp.concatenate([wrapped, value[:-1]], axis=0)


def z_next(halves, zero_edge):
    lane = lax.broadcasted_iota(jnp.int32, halves[0].shape, halves[0].ndim - 1)
    turned = [pltpu.roll(half, 127, half.ndim - 1) for half in halves]
    last = jnp.where(lane == 127, 0.0, turned[1]) if zero_edge else turned[1]
    return [jnp.where(lane == 127, turned[1], turned[0]), last]


def z_prev(halves, zero_edge):
    lane = lax.broadcasted_iota(jnp.int32, halves[0].shape, halves[0].ndim - 1)
    turned = [pltpu.roll(half, 1, half.ndim - 1) for half in halves]
    first = jnp.where(lane == 0, 0.0, turned[0]) if zero_edge else turned[0]
    return [first, jnp.where(lane == 0, turned[0], turned[1])]


def three_parts(value):
    high = value.astype(BF16)
    rest = value - high.astype(F32)
    middle = rest.astype(BF16)
    low = (rest - middle.astype(F32)).astype(BF16)
    return high.astype(F32), middle.astype(F32), low.astype(F32)


def kernel(
    groups,
    slabs,
    kappa,
    mua,
    prior_fwd,
    prior_adj,
    position,
    det_scalar,
    det_row,
    row_source,
    row_detector,
    row_data,
    row_weight,
    out,
    kap,
    mu,
    fwd_in,
    adj_in,
    field,
    other,
    adjf,
    coef,
    drive,
    agg,
    agg_in,
    val,
    val_in,
    det_in,
    zhot,
    picked,
    grad,
    grad_in,
    local_sem,
    halo_send,
    halo_recv,
    det_send,
    det_recv,
    agg_send,
    agg_recv,
    val_send,
    val_recv,
    grad_send,
    grad_recv,
):
    src = lax.axis_index("src")
    vox = lax.axis_index("vox")
    core = lax.rem(vox, 2)
    depth = kappa.shape[0]
    total = LOW + depth + HIGH
    detectors = det_row.shape[1]
    has_low = vox > 0
    has_high = vox < slabs - 1
    below = {"vox": jnp.maximum(vox - 1, 0)}
    above = {"vox": jnp.minimum(vox + 1, slabs - 1)}
    row, side = src // 2, lax.rem(src, 2)
    peers = [
        lax.rem(row + down, groups // 2) * 2 + lax.rem(side + across, 2)
        for down, across in ((2, 1), (1, 0), (3, 0), (2, 0), (1, 1), (3, 1), (0, 1))
    ]

    barrier = pltpu.get_barrier_semaphore()

    @pl.when(has_high)
    def _():
        pl.semaphore_signal(barrier, inc=1, device_id=above, device_id_type=MESH)

    @pl.when(has_low)
    def _():
        pl.semaphore_signal(barrier, inc=1, device_id=below, device_id_type=MESH)

    for peer in peers:
        pl.semaphore_signal(barrier, inc=1, device_id={"src": peer}, device_id_type=MESH)

    own = []
    for h in range(2):
        lanes = pl.ds(128 * h, 128)
        own.append(
            [
                pltpu.make_async_copy(
                    kappa.at[:, :, lanes], kap.at[pl.ds(LOW, depth), h], local_sem.at[0, h]
                ),
                pltpu.make_async_copy(
                    mua.at[:, :, lanes], mu.at[pl.ds(LOW, depth), h], local_sem.at[1, h]
                ),
                pltpu.make_async_copy(
                    prior_fwd.at[:, :, :, lanes],
                    fwd_in.at[:, pl.ds(LOW, depth), h],
                    local_sem.at[2, h],
                ),
                pltpu.make_async_copy(
                    prior_adj.at[:, :, :, lanes],
                    adj_in.at[:, pl.ds(LOW, depth), h],
                    local_sem.at[3, h],
                ),
            ]
        )
    for which in range(4):
        for h in range(2):
            own[h][which].start()

    pl.semaphore_wait(
        barrier, groups - 1 + jnp.where(has_low, 1, 0) + jnp.where(has_high, 1, 0)
    )

    def halo(array, direction, h):
        lanes = pl.ds(128 * h, 128)
        if direction == 0:
            count = LOW - 1 if array == 1 else LOW
            start, target = depth - count, LOW - count
        else:
            count = HIGH - 1 if array == 1 else HIGH
            start, target = 0, LOW + depth
        if array < 2:
            source = (kappa, mua)[array].at[pl.ds(start, count), :, lanes]
            place = (kap, mu)[array].at[pl.ds(target, count), h]
        else:
            source = (prior_fwd, prior_adj)[array - 2].at[:, pl.ds(start, count), :, lanes]
            place = (fwd_in, adj_in)[array - 2].at[:, pl.ds(target, count), h]
        return pltpu.make_async_remote_copy(
            src_ref=source,
            dst_ref=place,
            send_sem=halo_send.at[array, direction, h],
            recv_sem=halo_recv.at[array, direction, h],
            device_id=above if direction == 0 else below,
            device_id_type=MESH,
        )

    halos = [[[halo(a, d, h) for h in range(2)] for d in range(2)] for a in range(4)]
    det_copy = [
        pltpu.make_async_remote_copy(
            src_ref=det_row,
            dst_ref=det_in.at[d],
            send_sem=det_send.at[d],
            recv_sem=det_recv.at[d],
            device_id=(above, below)[d],
            device_id_type=MESH,
        )
        for d in range(2)
    ]

    sends_to = (has_high, has_low)
    gets_from = (has_low, has_high)
    for d in range(2):

        @pl.when(sends_to[d])
        def _():
            det_copy[d].start()
            for a in range(4):
                for h in range(2):
                    halos[a][d][h].start()

    for d in range(2):

        @pl.when(jnp.logical_not(gets_from[d]))
        def _():
            if d == 0:
                planes = slice(0, LOW)
            else:
                planes = slice(LOW + depth, total)
            kap[planes] = jnp.zeros_like(kap[planes])
            fwd_in[:, planes] = jnp.zeros_like(fwd_in[:, planes])
            adj_in[:, planes] = jnp.zeros_like(adj_in[:, planes])
            det_in[d] = jnp.zeros_like(det_in[d])
            val_in[d] = jnp.zeros_like(val_in[d])

    rows = lax.broadcasted_iota(jnp.int32, (8 * groups, 128), 0)
    kind = rows % 8
    source_of = rows // 8 * 2 + kind % 2
    det_base = vox * detectors
    det_ids = lax.broadcasted_iota(jnp.int32, (detectors, 128), 0) + det_base
    summed = jnp.zeros((8 * groups, detectors), F32)
    for i in range(row_source.shape[0]):
        weight = row_weight[i : i + 1, :]
        weighted = weight * row_data[i : i + 1, :]
        chosen = jnp.where(kind < 2, weight, jnp.where(kind < 4, weighted, 0.0))
        chosen = jnp.where(row_source[i : i + 1, :] == source_of, chosen, 0.0)
        hot = jnp.where(row_detector[i : i + 1, :] == det_ids, 1.0, 0.0)
        summed = summed + lax.dot_general(
            chosen, hot, NT, precision=HI, preferred_element_type=F32
        )
    agg[...] = summed
    agg_copy = []
    for step, peer in enumerate(peers):
        copy = pltpu.make_async_remote_copy(
            src_ref=agg.at[pl.ds(pl.multiple_of(8 * peer, 8), 8)],
            dst_ref=agg_in.at[src],
            send_sem=agg_send.at[step],
            recv_sem=agg_recv.at[step],
            device_id={"src": peer},
            device_id_type=MESH,
        )
        copy.start()
        agg_copy.append(copy)
    agg_in[src] = agg[pl.ds(pl.multiple_of(8 * src, 8), 8), :]

    def coefficients(low, count):
        def body(i, carry):
            p = low + i
            x = vox * depth + p - LOW
            inside = jnp.logical_and(x >= 0, x < slabs * depth)
            centre = [slots(kap, p, h) for h in range(2)]
            zn, zp = z_next(centre, True), z_prev(centre, True)
            row = lax.broadcasted_iota(jnp.int32, (8, 8, 128), 1) * 8 + lax.broadcasted_iota(
                jnp.int32, (8, 8, 128), 0
            )
            lane = lax.broadcasted_iota(jnp.int32, (8, 8, 128), 2)
            for h in range(2):
                mid = centre[h]
                faces = [
                    0.5 * (slots(kap, p + 1, h) + mid),
                    0.5 * (mid + slots(kap, p - 1, h)),
                    0.5 * (y_next(mid, True) + mid),
                    0.5 * (mid + y_prev(mid, True)),
                    0.5 * (zn[h] + mid),
                    0.5 * (mid + zp[h]),
                ]
                diagonal = slots(mu, p, h)
                for face in faces:
                    diagonal = diagonal + face
                inverse = jnp.where(inside, 1.0 / jnp.where(inside, diagonal, 1.0), 0.0)
                faces[2] = jnp.where(row == 63, 0.0, faces[2])
                faces[3] = jnp.where(row == 0, 0.0, faces[3])
                if h == 1:
                    faces[4] = jnp.where(lane == 127, 0.0, faces[4])
                else:
                    faces[5] = jnp.where(lane == 0, 0.0, faces[5])
                for n in range(6):
                    coef[n, p - 1, h] = faces[n] * inverse
                coef[6, p - 1, h] = inverse
                cell = (x * 64 + row) * 256 + 128 * h + lane
                for s in range(2):
                    spot = position[src * 2 + s]
                    drive[p - 1, s, h] = jnp.where(cell == spot, source_gain * inverse, 0.0)
            return carry

        lax.fori_loop(0, count, body, 0)

    def take_in(source, place, low, count):
        def body(i, carry):
            p = low + i
            for s in range(2):
                for h in range(2):
                    place[p, s, h] = slots(source, s, p, h)
            return carry

        lax.fori_loop(0, count, body, 0)

    def sweep(old, new, low, count):
        def body(i, carry):
            p = low + i
            for s in range(2):
                centre = [old[p, s, h] for h in range(2)]
                zn, zp = z_next(centre, False), z_prev(centre, False)
                for h in range(2):
                    mid = centre[h]
                    value = drive[p - 1, s, h] + coef[0, p - 1, h] * old[p + 1, s, h]
                    value = value + coef[1, p - 1, h] * old[p - 1, s, h]
                    value = value + coef[2, p - 1, h] * y_next(mid, False)
                    value = value + coef[3, p - 1, h] * y_prev(mid, False)
                    value = value + coef[4, p - 1, h] * zn[h]
                    value = value + coef[5, p - 1, h] * zp[h]
                    new[p, s, h] = value
            return carry

        lax.fori_loop(0, count, body, 0)

    def pick(even, odd):
        return jnp.where(core == 0, even, odd)

    def early(k):
        return pick(k, k - LOW) + LOW, pick(depth + LOW + 1 - 2 * k, depth + LOW - 2 * k)

    def late(k):
        return pick(k - LOW, depth - k) + LOW, pick(LOW, LOW + 1)

    def solve(fields, part):
        for k in range(1, SWEEPS + 1):
            low, count = part(k)
            sweep(fields[(k - 1) % 2], fields[k % 2], low, count)

    def await_halo(arrays, near):
        for d in range(2):
            on_core = (1 - d) if near else d
            wanted = jnp.logical_and(core == on_core, gets_from[d])

            @pl.when(wanted)
            def _():
                for a in arrays:
                    for h in range(2):
                        halos[a][d][h].wait_recv()

    for which in range(4):
        for h in range(2):
            own[h][which].wait()
    await_halo((0, 1), True)
    near_low = pick(1, 1 - LOW) + LOW
    near_count = pick(depth + LOW - 1, depth + LOW - 2)
    far_low = pick(1 - LOW, depth - 1) + LOW
    far_count = pick(LOW, LOW + 1)
    coefficients(near_low, near_count)
    await_halo((2,), True)
    take_in(fwd_in, field, pick(0, -LOW) + LOW, pick(depth + HIGH, depth + LOW))
    solve((field, other), early)
    await_halo((3,), True)
    take_in(adj_in, adjf, pick(0, -LOW) + LOW, pick(depth + HIGH, depth + LOW))

    identity = jnp.where(
        lax.broadcasted_iota(jnp.int32, (detectors, 128), 0)
        == lax.broadcasted_iota(jnp.int32, (detectors, 128), 1),
        1.0,
        0.0,
    )
    for d in range(2):

        @pl.when(gets_from[d])
        def _():
            det_copy[d].wait_recv()

    for n in range(3):
        where_row = det_in[n] if n < 2 else det_row[...]
        z_row = jnp.broadcast_to((where_row % 256).astype(F32), (8, detectors))
        z_col = lax.dot_general(identity, z_row, NT, precision=HI, preferred_element_type=F32)
        lane = lax.broadcasted_iota(jnp.int32, (detectors, 256), 1).astype(F32)
        zhot[n] = jnp.where(lane == z_col[:, :1], 1.0, 0.0)

    await_halo((0, 1), False)
    coefficients(far_low, far_count)
    await_halo((2,), False)
    take_in(fwd_in, field, pick(-LOW, depth) + LOW, pick(LOW, HIGH))
    solve((field, other), late)

    def gather(d, carry):
        spot = det_scalar[d] - vox * (depth * 64 * 256)
        spot = jnp.clip(spot, 0, depth * 64 * 256 - 1)
        p = lax.shift_right_logical(spot, 14)
        row = lax.shift_right_logical(spot, 8)
        slot = lax.bitwise_and(row, 7)
        sublane = lax.bitwise_and(lax.shift_right_logical(row, 3), 7)
        for s in range(2):
            for h in range(2):
                picked[s, h, pl.ds(d, 1), :] = field[p + LOW, s, h, slot, pl.ds(sublane, 1), :]
        return carry

    lax.fori_loop(0, detectors, gather, 0, unroll=4)
    for copy in agg_copy:
        copy.wait()
    sums = agg_in[0]
    for g in range(1, groups):
        sums = sums + agg_in[g]
    predicted = []
    for s in range(2):
        both = picked[s, 0] * zhot[2, :, :128] + picked[s, 1] * zhot[2, :, 128:]
        predicted.append(
            lax.dot_general(
                jnp.ones((8, 128), F32), both, NT, precision=HI, preferred_element_type=F32
            )
        )
    rows8 = lax.broadcasted_iota(jnp.int32, (8, detectors), 0)
    val[...] = sums * jnp.where(rows8 == 0, predicted[0], predicted[1]) - pltpu.roll(sums, 6, 0)
    val_copy = [
        pltpu.make_async_remote_copy(
            src_ref=val,
            dst_ref=val_in.at[d],
            send_sem=val_send.at[d],
            recv_sem=val_recv.at[d],
            device_id=(above, below)[d],
            device_id_type=MESH,
        )
        for d in range(2)
    ]
    for d in range(2):

        @pl.when(sends_to[d])
        def _():
            val_copy[d].start()

    def place_totals(n, totals, where_row, base, low, count):
        spot = where_row - (vox * depth + base) * (64 * 256)
        y = spot // 256 % 64
        code = spot // (64 * 256) * 64 + y % 8 * 8 + y // 8
        parts = [three_parts(totals[s : s + 1]) for s in range(2)]
        hot = zhot[n].astype(BF16)
        hot = jnp.concatenate([hot, hot, hot], axis=0)

        def body(i, carry):
            p = low + i
            rows64 = lax.broadcasted_iota(jnp.int32, (64, detectors), 0) + (p - base) * 64
            match = rows64 == code
            for s in range(2):
                left = [jnp.where(match, part, 0.0).astype(BF16) for part in parts[s]]
                value = lax.dot_general(
                    jnp.concatenate(left, axis=1),
                    hot,
                    (((1,), (0,)), ((), ())),
                    preferred_element_type=F32,
                )
                for h in range(2):
                    half = value[:, 128 * h : 128 * h + 128].reshape(8, 8, 128)
                    drive[p + LOW - 1, s, h] = half * coef[6, p + LOW - 1, h]
            return carry

        lax.fori_loop(0, count, body, 0)

    place_totals(2, val[...], det_row[...], 0, 0, depth)

    def await_values(near):
        for d in range(2):
            on_core = (1 - d) if near else d

            @pl.when(core == on_core)
            def _():
                @pl.when(gets_from[d])
                def _():
                    val_copy[d].wait_recv()

                if d == 0:
                    place_totals(0, val_in[0], det_in[0], -depth, 1 - LOW, LOW - 1)
                else:
                    place_totals(1, val_in[1], det_in[1], depth, depth, HIGH - 1)

    await_values(True)
    solve((adjf, other), early)
    await_values(False)
    await_halo((3,), False)
    take_in(adj_in, adjf, pick(-LOW, depth) + LOW, pick(LOW, HIGH))

    def stage(j):
        if j == 0:
            return lambda k: (pick(k, depth - k) + LOW, pick(0, 1))
        return lambda k: (pick(k - 2 * j, depth - 1 - k + 2 * j) + LOW, 2)

    tile = 64 // groups

    def gradient(i, carry):
        p = i + LOW
        mua_sum = [jnp.zeros((8, 8, 128), F32) for _ in range(2)]
        kap_sum = [jnp.zeros((8, 8, 128), F32) for _ in range(2)]
        for s in range(2):
            f = [field[p, s, h] for h in range(2)]
            a = [adjf[p, s, h] for h in range(2)]
            fz, az = z_next(f, True), z_next(a, True)
            for h in range(2):
                mua_sum[h] = mua_sum[h] - f[h] * a[h]
                product = (field[p + 1, s, h] - f[h]) * (adjf[p + 1, s, h] - a[h])
                product = product + (y_next(f[h], True) - f[h]) * (y_next(a[h], True) - a[h])
                product = product + (fz[h] - f[h]) * (az[h] - a[h])
                kap_sum[h] = kap_sum[h] - product
        for h in range(2):
            for j in range(8):
                grad[0, i, h, pl.ds(j, 8, stride=8), :] = mua_sum[h][j]
                grad[1, i, h, pl.ds(j, 8, stride=8), :] = kap_sum[h][j]
        return carry

    grad_copy = []
    for part in range(depth // 2):
        solve((adjf, other), stage(part))
        first = pick(depth - 2 - 2 * part, 2 * part)
        lax.fori_loop(first, first + 2, gradient, 0)
        planes = pl.ds(first, 2)
        for step, peer in enumerate(peers):
            copy = pltpu.make_async_remote_copy(
                src_ref=grad.at[:, planes, :, pl.ds(pl.multiple_of(tile * peer, 8), tile)],
                dst_ref=grad_in.at[step, :, planes],
                send_sem=grad_send.at[part, step],
                recv_sem=grad_recv.at[part, step],
                device_id={"src": peer},
                device_id_type=MESH,
            )
            copy.start()
            grad_copy.append(copy)

    for d in range(2):

        @pl.when(sends_to[d])
        def _():
            det_copy[d].wait_send()
            val_copy[d].wait_send()
            for a in range(4):
                for h in range(2):
                    halos[a][d][h].wait_send()

    for copy in grad_copy:
        copy.wait()
    mine = pl.ds(pl.multiple_of(tile * src, 8), tile)
    for q in range(2):
        for h in range(2):
            value = grad[q, :, h, mine, :]
            for step in range(groups - 1):
                value = value + grad_in[step, q, :, h]
            out[q, :, :, 128 * h : 128 * h + 128] = value


def body(
    kappa,
    mua,
    prior_forward_fields,
    prior_adjoint_fields,
    source_position,
    detector_voxel,
    measured_source,
    measured_detector,
    measured_data,
    measured_weight,
):
    groups = lax.axis_size("src")
    slabs = lax.axis_size("vox")
    depth, width, _ = kappa.shape
    total = LOW + depth + HIGH
    detectors = detector_voxel.shape[0]
    blocks = (-1, 128)
    hbm = pl.BlockSpec(memory_space=pl.ANY)
    vmem = pl.BlockSpec(memory_space=pltpu.VMEM)
    smem = pl.BlockSpec(memory_space=pltpu.SMEM)
    tile = width // groups
    dma = pltpu.SemaphoreType.DMA
    slab_field = pltpu.VMEM((total, 2, 2, 8, 8, 128), F32)
    both = pl.pallas_call(
        functools.partial(kernel, groups, slabs),
        out_shape=jax.ShapeDtypeStruct((2, depth, tile, 256), F32),
        in_specs=[hbm] * 4 + [smem] * 2 + [vmem] * 5,
        out_specs=vmem,
        scratch_shapes=[
            pltpu.VMEM((total, 2, 64, 128), F32),
            pltpu.VMEM((total, 2, 64, 128), F32),
            pltpu.VMEM((2, total, 2, 64, 128), F32),
            pltpu.VMEM((2, total, 2, 64, 128), F32),
            slab_field,
            slab_field,
            slab_field,
            pltpu.VMEM((7, total - 2, 2, 8, 8, 128), F32),
            pltpu.VMEM((total - 2, 2, 2, 8, 8, 128), F32),
            pltpu.VMEM((8 * groups, detectors), F32),
            pltpu.VMEM((groups, 8, detectors), F32),
            pltpu.VMEM((8, detectors), F32),
            pltpu.VMEM((2, 8, detectors), F32),
            pltpu.VMEM((2, 1, detectors), jnp.int32),
            pltpu.VMEM((3, detectors, 256), F32),
            pltpu.VMEM((2, 2, detectors, 128), F32),
            pltpu.VMEM((2, depth, 2, 64, 128), F32),
            pltpu.VMEM((groups - 1, 2, depth, 2, tile, 128), F32),
            dma((4, 2)),
            dma((4, 2, 2)),
            dma((4, 2, 2)),
            dma((2,)),
            dma((2,)),
            dma((groups - 1,)),
            dma((groups - 1,)),
            dma((2,)),
            dma((2,)),
            dma((depth // 2, groups - 1)),
            dma((depth // 2, groups - 1)),
        ],
        compiler_params=pltpu.CompilerParams(
            collective_id=0, has_side_effects=True, vmem_limit_bytes=60000 * 1024
        ),
        name="tomography",
    )(
        kappa,
        mua,
        prior_forward_fields,
        prior_adjoint_fields,
        source_position,
        detector_voxel,
        detector_voxel.reshape(1, detectors),
        measured_source.reshape(blocks),
        measured_detector.reshape(blocks),
        measured_data.reshape(blocks),
        measured_weight.reshape(blocks),
    )
    return both[0], both[1]


def solution(mesh):
    in_specs = (
        P("vox", None, None),
        P("vox", None, None),
        P("src", "vox", None, None),
        P("src", "vox", None, None),
        P(),
        P("vox"),
        P(("src", "vox")),
        P(("src", "vox")),
        P(("src", "vox")),
        P(("src", "vox")),
    )
    out_specs = (P("vox", "src", None), P("vox", "src", None))
    return jax.shard_map(body, mesh=mesh, in_specs=in_specs, out_specs=out_specs, check_vma=False)
```
